768 devices in a mesh: lon: 64 (over x, y, core), lat: 12 (over z).
Axes of the slice: x: 4, y: 8, z: 12, core: 2. Of those that a mesh axis runs over, the one named last changes fastest.
Arguments:
- state_prev: float32 [7, 16, 192, 8192], P(None, None, 'lat', 'lon'), may hold values from -6 to 6
- state_now: float32 [7, 16, 192, 8192], P(None, None, 'lat', 'lon'), may hold values from -6 to 6
- stride_table: int32 [192], P('lat'), may hold values from 1 to 32, as said below
- filter_len: int32 [192], P('lat'), may hold values from 1 to 32, as said below
- zonal_coef: float32 [192], P('lat'), may hold values from 0.05 to 0.3
- merid_coef: float32 [16], replicated, may hold values from 0.05 to 0.3
- filter_coef: float32 [16], replicated, may hold values from 0.03 to 0.2
- w_first: bfloat16 [7, 64], replicated, may hold values from -2 to 2
- b_first: float32 [64], replicated, may hold values from -3 to 3
- w_second: bfloat16 [64, 64], replicated, may hold values from -0.75 to 0.75
- b_second: float32 [64], replicated, may hold values from -3 to 3
- w_third: bfloat16 [64, 224], replicated, may hold values from -0.75 to 0.75
- b_third: float32 [224], replicated, may hold values from -3 to 3
- band_weight: float32 [224], replicated, may hold values from 0.02 to 0.2
- sunlit_cols: int32 [12, 64, 1536], P('lat', 'lon'), may hold values from 0 to 2047, as said below
- sunlit_count: int32 [12, 64], P('lat'), may hold values from 0 to 1536, as said below
Outputs:
- prev_out: float32 [7, 16, 192, 8192], P(None, None, 'lat', 'lon')
- now_out: float32 [7, 16, 192, 8192], P(None, None, 'lat', 'lon')
The draws below stay inside these ranges and needn't reach their ends.
Inputs may be any that keep to these rules, and one draw needn't show every extreme that they name: `stride_table`: 1 except in the 4 rows nearest each end of the latitude range. `filter_len`: 1 except in the 4 rows nearest each end of the latitude range. `sunlit_cols`: the entries of one device's list are distinct. `sunlit_count`: a device's count plus that of the device 64 / 2 further along lon (cyclic) in the same band is at most 1536.
All inputs are finite; a program needn't handle non-finite values.
Results may differ from the reference program's by a relative error of at most 0.0003.
Values may be sent and summed in bfloat16 or wider, within the bound.
No kernel may reach another device: no remote copies, remote signals or barrier semaphores. Data moves between devices by JAX's collectives and lax.ppermute only.
A program may use at most 64 MiB of HBM per device.

```python
import math
import jax
import jax.numpy as jnp
from jax import lax

CLON = 128
CLAT = 16
LEV = 16
VARS = 7
HID = 64
GPT = 224
SMAX = 32
POLAR = 4
RCOL = 1536
NLON = 8192
NLAT = 192
N_LON = 64
N_LAT = 12


def polar_table(key, salt):
    rows = jnp.arange(NLAT, dtype=jnp.int32)
    dist = jnp.minimum(rows, NLAT - 1 - rows)
    values = jax.random.randint(jax.random.fold_in(key, salt), (NLAT,), 1, SMAX + 1, dtype=jnp.int32)
    values = jnp.where(dist == 0, SMAX, values)
    return jnp.where(dist < POLAR, values, 1).astype(jnp.int32)


def draw_stride_table(key, part):
    return polar_table(key, 11)


def draw_filter_len(key, part):
    return polar_table(key, 23)


def draw_sunlit_cols(key, part):
    keys = jax.random.split(jax.random.fold_in(key, 37), N_LAT * N_LON)
    lists = jax.vmap(lambda k: jax.random.permutation(k, CLAT * CLON)[:RCOL])(keys)
    return lists.reshape(N_LAT, N_LON, RCOL).astype(jnp.int32)


def draw_sunlit_count(key, part):
    half = N_LON // 2
    base = jax.random.fold_in(key, 53)
    day = jax.random.randint(jax.random.fold_in(base, 1), (N_LAT, half), RCOL // 2, RCOL + 1, dtype=jnp.int32)
    pairs = jnp.arange(half, dtype=jnp.int32)
    day = jnp.where(pairs[None, :] == 0, RCOL, day)
    spare = RCOL - day
    night = jax.random.randint(jax.random.fold_in(base, 2), (N_LAT, half), 0, RCOL + 1, dtype=jnp.int32) % (spare + 1)
    flip = jax.random.randint(jax.random.fold_in(base, 3), (N_LAT, half), 0, 2, dtype=jnp.int32)
    first = jnp.where(flip == 1, day, night)
    second = jnp.where(flip == 1, night, day)
    return jnp.concatenate([first, second], axis=1).astype(jnp.int32)


def steps_of(rng, dims, cuts, low, high):
    gain, own = 1.0, jax.random.fold_in(rng, 6)
    for position, parts in cuts:
        draws = jnp.exp(jax.random.uniform(jax.random.fold_in(own, position), (parts,), jnp.float32, low / len(cuts), high / len(cuts)))
        gain = gain * jnp.repeat(draws, dims[position] // parts).reshape([-1 if axis == position else 1 for axis in range(len(dims))])
    return gain


def bell_draw(stream_key, shape, spread, most, cuts=(), kind=jnp.bfloat16):
    array = spread * jax.random.normal(stream_key, shape, jnp.float32)
    if cuts:
        array = array * steps_of(stream_key, shape, cuts, -0.22, 0.18)
    return jnp.clip(array, -most, most).astype(kind)


def setup_inputs(seed: int = 0) -> dict:
    arg_keys = jax.random.split(jax.random.key(seed), 17)
    return {
        "state_prev": bell_draw(arg_keys[0], (VARS, LEV, NLAT, NLON), 1.0, 6.0, ((2, 12), (3, 64)), jnp.float32),
        "state_now": bell_draw(arg_keys[1], (VARS, LEV, NLAT, NLON), 1.0, 6.0, ((2, 12), (3, 64)), jnp.float32),
        "stride_table": draw_stride_table(jax.random.fold_in(arg_keys[16], 71), 0),
        "filter_len": draw_filter_len(jax.random.fold_in(arg_keys[16], 71), 0),
        "zonal_coef": jnp.clip(jnp.exp(math.log(0.3) - 1.7917595 * jax.random.uniform(arg_keys[4], (NLAT,), jnp.float32) ** steps_of(arg_keys[4], (NLAT,), ((0, 12),), -0.2, 0.2)), 0.05, 0.3),
        "merid_coef": jnp.clip(jnp.exp(jax.random.uniform(arg_keys[5], (LEV,), jnp.float32, math.log(0.05), math.log(0.3))), 0.05, 0.3),
        "filter_coef": jnp.clip(jnp.exp(jax.random.uniform(arg_keys[6], (LEV,), jnp.float32, math.log(0.03), math.log(0.2))), 0.03, 0.2),
        "w_first": bell_draw(arg_keys[7], (VARS, HID), VARS ** -0.5, 2.0),
        "b_first": bell_draw(arg_keys[8], (HID,), 0.5, 3.0, (), jnp.float32),
        "w_second": bell_draw(arg_keys[9], (HID, HID), HID ** -0.5, 0.75),
        "b_second": bell_draw(arg_keys[10], (HID,), 0.5, 3.0, (), jnp.float32),
        "w_third": bell_draw(arg_keys[11], (HID, GPT), HID ** -0.5, 0.75),
        "b_third": bell_draw(arg_keys[12], (GPT,), 0.5, 3.0, (), jnp.float32),
        "band_weight": jnp.clip(jnp.exp(jax.random.uniform(arg_keys[13], (GPT,), jnp.float32, math.log(0.02), math.log(0.2))), 0.02, 0.2),
        "sunlit_cols": draw_sunlit_cols(jax.random.fold_in(arg_keys[16], 71), 0),
        "sunlit_count": draw_sunlit_count(jax.random.fold_in(arg_keys[16], 71), 0),
    }


def absorb(feats_t, w_first, b_first, w_second, b_second, w_third, b_third, band_weight):
    count = feats_t.shape[2]
    levels = feats_t.shape[1]
    rows = jnp.transpose(feats_t, (2, 1, 0)).reshape(count * levels, feats_t.shape[0])
    first = jax.nn.silu(jnp.dot(rows, w_first, preferred_element_type=jnp.float32) + b_first).astype(jnp.bfloat16)
    second = jax.nn.silu(jnp.dot(first, w_second, preferred_element_type=jnp.float32) + b_second).astype(jnp.bfloat16)
    tau = 0.15 * jax.nn.softplus(jnp.dot(second, w_third, preferred_element_type=jnp.float32) + b_third)
    tau = tau.reshape(count, levels, tau.shape[-1])
    depth = jnp.cumsum(tau, axis=1)
    above = depth - tau
    return jnp.sum((jnp.exp(-above) - jnp.exp(-depth)) * band_weight, axis=-1)


def step(prev, now, stride_table, filter_len, zonal_coef, merid_coef, filter_coef):
    width = now.shape[-1]
    cols = jnp.arange(width, dtype=jnp.int32)
    inv_s = 1.0 / stride_table.astype(jnp.float32)
    wind_u = now[0]
    wind_v = now[1]

    def pick(field, offset):
        index = (cols[None, :] + offset[:, None]) % width
        return jnp.take_along_axis(field, jnp.broadcast_to(index[None], field.shape), axis=2)

    def advance(pair):
        old, field = pair
        plus = pick(field, stride_table)
        minus = pick(field, -stride_table)
        fplus = pick(field, filter_len)
        fminus = pick(field, -filter_len)
        padded = jnp.pad(field, ((0, 0), (1, 1), (0, 0)))
        merid = padded[:, 2:] - padded[:, :-2]
        tend = -zonal_coef[None, :, None] * wind_u * ((plus - minus) * inv_s[None, :, None])
        tend = tend - merid_coef[:, None, None] * wind_v * merid
        tend = tend + filter_coef[:, None, None] * (fplus - 2.0 * field + fminus)
        return old + tend

    new = lax.map(advance, (prev, now))
    return now + 0.1 * (prev - 2.0 * now + new), new


def reference(state_prev, state_now, stride_table, filter_len, zonal_coef, merid_coef, filter_coef, w_first, b_first, w_second, b_second, w_third, b_third, band_weight, sunlit_cols, sunlit_count):
    prev, now = state_prev, state_now
    for turn in range(2):
        prev, now = step(prev, now, stride_table, filter_len, zonal_coef, merid_coef, filter_coef)
    devices = N_LAT * N_LON
    listed = sunlit_cols.reshape(devices, RCOL).astype(jnp.int32)
    which = jnp.arange(devices, dtype=jnp.int32)
    glat = (which // N_LON)[:, None] * CLAT + listed // CLON
    glon = (which % N_LON)[:, None] * CLON + listed % CLON
    counts = sunlit_count.reshape(devices).astype(jnp.int32)
    slots = jnp.arange(RCOL, dtype=jnp.int32)

    def one(args):
        rows_here, cols_here, live = args
        feats = now[:, :, rows_here, cols_here].astype(jnp.bfloat16)
        heat = absorb(feats, w_first, b_first, w_second, b_second, w_third, b_third, band_weight)
        return jnp.where((slots < live)[:, None], heat, jnp.float32(0.0))

    heats = lax.map(one, (glat, glon, counts))
    temper = now[2].at[:, glat.reshape(-1), glon.reshape(-1)].add(heats.reshape(-1, LEV).T)
    now_out = now.at[2].set(temper)
    return prev, now_out
```

```python
import functools

import jax
import jax.numpy as jnp
from jax import lax
from jax.experimental import pallas as pl
from jax.experimental.pallas import tpu as pltpu
from jax.sharding import PartitionSpec as P

VARS = 7
LEV = 16
ROWS = 16
LANES = 128
POLAR = 4
HID = 64
GPT = 224
LISTED = 1536
TILES_POLAR = VARS * LEV // 2
TILES_COLS = 16
LON_ROWS = 8 * (TILES_POLAR + TILES_COLS)
LAT_NOW = VARS * 4
LAT_PREV = VARS * 2
LAT_ROWS = 8 * (LAT_NOW + LAT_PREV + 1)
LOG2E = 1.4426950408889634
TAU_SCALE = 0.15

f32 = jnp.float32
bf16 = jnp.bfloat16


def iotas():
    lane = lax.broadcasted_iota(jnp.int32, (8, LANES), 1)
    sub = lax.broadcasted_iota(jnp.int32, (8, LANES), 0)
    return lane, sub


def roll_lanes(x, shift):
    return pltpu.roll(x, shift, 1)


def roll_subs(x, shift):
    return pltpu.roll(x, shift, 0)


def pick(x, index):
    return jnp.take_along_axis(x, index, axis=1, mode="promise_in_bounds")


def col_tile(which, half, group):
    return 8 * (TILES_POLAR + which * 8 + half * 4 + group)


def pack_kernel(first_ref, now_ref, prev_ref, zc_ref, east_ref, west_ref, north_ref, south_ref):
    lane, sub = iotas()
    first = first_ref[0]
    base = pl.multiple_of(jnp.where(first == 1, 0, 8), 8)
    turn = jnp.where(first == 1, 0, 4)
    extra = jnp.where(first == 1, 4, 11)

    def polar(k, carry):
        for v in range(VARS):
            east = []
            west = []
            for part in range(2):
                level = k + 8 * part
                amount = (4 * part + turn) % 8
                tile = roll_subs(now_ref[v, level, pl.ds(base, 8), :], amount)
                old = roll_lanes(roll_subs(prev_ref[v, level, pl.ds(base, 8), :], amount), 64)
                row = jnp.broadcast_to(now_ref[v, level, pl.ds(extra, 1), :], (8, LANES))
                east.append(
                    jnp.where(lane >= 64, tile, jnp.where(lane >= 32, old, roll_lanes(row, 32)))
                )
                west.append(
                    jnp.where(lane < 64, tile, jnp.where(lane < 96, old, roll_lanes(row, 96)))
                )
            at = pl.multiple_of((v * 8 + k) * 8, 8)
            east_ref[pl.ds(at, 8), :] = jnp.where(sub < 4, east[0], east[1])
            west_ref[pl.ds(at, 8), :] = jnp.where(sub < 4, west[0], west[1])
        return carry

    lax.fori_loop(0, 8, polar, 0)

    for group in range(4):
        members = [v for v in (2 * group, 2 * group + 1) if v < VARS]

        def columns(k, tiles):
            tiles = list(tiles)
            for v in members:
                at = (v % 2) * 64 + 4 * k
                low = (lane == at) | (lane == at + 1)
                high = (lane == at + 2) | (lane == at + 3)
                for which, ref in enumerate((now_ref, prev_ref)):
                    for half in range(2):
                        x = ref[v, k, pl.ds(8 * half, 8), :]
                        slot = 4 * which + 2 * half
                        tiles[slot] = jnp.where(low, roll_lanes(x, at), tiles[slot])
                        tiles[slot + 1] = jnp.where(
                            high, roll_lanes(x, (at + 4) % LANES), tiles[slot + 1]
                        )
            return tuple(tiles)

        zero = jnp.zeros((8, LANES), f32)
        tiles = lax.fori_loop(0, LEV, columns, (zero,) * 8)
        for which in range(2):
            for half in range(2):
                at = col_tile(which, half, group)
                west_ref[at : at + 8, :] = tiles[4 * which + 2 * half]
                east_ref[at : at + 8, :] = tiles[4 * which + 2 * half + 1]

    def rows_now(g, carry):
        for v in range(VARS):
            north = None
            south = None
            for h in range(4):
                up = now_ref[v, g + 4 * h, 0:8, :]
                down = now_ref[v, g + 4 * h, 8:16, :]
                up = roll_subs(up, 2 * h) if h else up
                down = roll_subs(down, (2 * h + 2) % 8) if h != 3 else down
                mask = sub >= 2 * h
                north = up if h == 0 else jnp.where(mask, up, north)
                south = down if h == 0 else jnp.where(mask, down, south)
            at = pl.multiple_of((v * 4 + g) * 8, 8)
            north_ref[pl.ds(at, 8), :] = north
            south_ref[pl.ds(at, 8), :] = south
        return carry

    lax.fori_loop(0, 4, rows_now, 0)

    def rows_prev(g, carry):
        for v in range(VARS):
            north = None
            south = None
            for h in range(8):
                up = prev_ref[v, g + 2 * h, 0:8, :]
                down = prev_ref[v, g + 2 * h, 8:16, :]
                up = roll_subs(up, h) if h else up
                down = roll_subs(down, h + 1) if h != 7 else down
                mask = sub >= h
                north = up if h == 0 else jnp.where(mask, up, north)
                south = down if h == 0 else jnp.where(mask, down, south)
            at = pl.multiple_of((LAT_NOW + v * 2 + g) * 8, 8)
            north_ref[pl.ds(at, 8), :] = north
            south_ref[pl.ds(at, 8), :] = south
        return carry

    lax.fori_loop(0, 2, rows_prev, 0)
    north_ref[LAT_ROWS - 8 :, :] = jnp.broadcast_to(zc_ref[0:1, :], (8, LANES))
    south_ref[LAT_ROWS - 8 :, :] = jnp.broadcast_to(zc_ref[15:16, :], (8, LANES))


def main_kernel(
    first_ref,
    count_ref,
    merid_ref,
    filter_ref,
    now_ref,
    prev_ref,
    fromwest_ref,
    fromeast_ref,
    fromnorth_ref,
    fromsouth_ref,
    stride_ref,
    flen_ref,
    zc_ref,
    listed_ref,
    w1_ref,
    b1_ref,
    w2_ref,
    b2_ref,
    w3_ref,
    b3_ref,
    start_ref,
    prev_out,
    now_out,
    outp_ref,
    outn_ref,
    feats_ref,
    pstar_ref,
    h1_ref,
    h2_ref,
    part_ref,
    mask_ref,
    sems,
    last_sem,
):
    lane, sub = iotas()
    first = first_ref[0]
    polar_base = jnp.where(first == 1, 0, 4)
    east_cols = (lane % 4) < 2
    for i in range(TILES_COLS):
        at = 8 * (TILES_POLAR + i)
        pstar_ref[8 * i : 8 * i + 8, :] = jnp.where(
            east_cols, fromeast_ref[at : at + 8, :], fromwest_ref[at : at + 8, :]
        )
    corner = []
    for group in range(4):
        at = LAT_ROWS - 8 + group
        corner.append(
            jnp.where(
                sub == 7,
                jnp.broadcast_to(fromnorth_ref[at : at + 1, :], (8, LANES)),
                jnp.broadcast_to(fromsouth_ref[at : at + 1, :], (8, LANES)),
            )
        )
    at = LAT_ROWS - 4
    zc_outer = jnp.where(
        sub == 7,
        jnp.broadcast_to(fromnorth_ref[at : at + 1, :], (8, LANES)),
        jnp.broadcast_to(fromsouth_ref[at : at + 1, :], (8, LANES)),
    )
    col_offset = jnp.where(
        lane < 64, jnp.minimum(lane, 1), jnp.maximum(lane, 126) - 124
    )
    edge = (lane < 2) | (lane >= 126)
    usecol = [edge | (first != 1), edge | (first == 1)]
    is_polar = (sub >= polar_base) & (sub < polar_base + 4)
    swap = jnp.where(lane < 64, lane + 96, lane - 96) % LANES

    def shifts(amount):
        return (
            (lane + amount) % LANES,
            lane < amount,
            (lane - amount) % LANES,
            lane >= LANES - amount,
        )

    s_tab = [shifts(stride_ref[0:8, :]), shifts(stride_ref[8:16, :])]
    m_tab = [shifts(flen_ref[0:8, :]), shifts(flen_ref[8:16, :])]
    one_tab = shifts(jnp.ones((8, LANES), jnp.int32))
    cz = [
        zc_ref[0:8, :] * (1.0 / stride_ref[0:8, :].astype(f32)),
        zc_ref[8:16, :] * (1.0 / stride_ref[8:16, :].astype(f32)),
    ]

    def ahead(x, other, tab):
        return pick(jnp.where(tab[1], other, x), tab[0])

    def behind(x, other, tab):
        return pick(jnp.where(tab[3], other, x), tab[2])

    def merid_of(t0, t1, t2, last):
        u0, u1, u2 = (roll_subs(t, 7) for t in (t0, t1, t2))
        d0, d1, d2 = (roll_subs(t, 1) for t in (t0, t1, t2))
        bottom = sub == 7
        top = sub == 0
        out = [
            jnp.where(bottom, u1, u0) - jnp.where(top, d2, d0),
            jnp.where(bottom, u2, u1) - jnp.where(top, d0, d1),
        ]
        if last:
            out.append(jnp.where(bottom, u0, u2) - jnp.where(top, d1, d2))
        return out

    def level(k, carry):
        mc = merid_ref[k]
        fc = filter_ref[k]
        pol_at = 8 * (k % 8)
        pol_turn = (polar_base + 8 - 4 * (k // 8)) % 8
        gn, hn = k % 4, k // 4
        gp, hp = k % 2, k // 2

        def gather_tiles(v):
            group = v // 2
            index = col_offset + (v % 2) * 64 + 4 * k
            cells = [now_ref[v, k, 0:8, :], now_ref[v, k, 8:16, :]]
            old = [prev_ref[v, k, 0:8, :], prev_ref[v, k, 8:16, :]]
            at = pl.multiple_of((v * 4 + gn) * 8, 8)
            t2 = jnp.where(
                sub >= 4,
                roll_subs(fromnorth_ref[pl.ds(at, 8), :], (14 - 2 * hn) % 8),
                roll_subs(fromsouth_ref[pl.ds(at, 8), :], (8 - 2 * hn) % 8),
            )
            at = pl.multiple_of((LAT_NOW + v * 2 + gp) * 8, 8)
            t2_old = jnp.where(
                sub >= 4,
                roll_subs(fromnorth_ref[pl.ds(at, 8), :], 7 - hp),
                roll_subs(fromsouth_ref[pl.ds(at, 8), :], (8 - hp) % 8),
            )
            at = pl.multiple_of(v * 64 + pol_at, 8)
            te = fromeast_ref[pl.ds(at, 8), :]
            tw = fromwest_ref[pl.ds(at, 8), :]
            natural = roll_subs(jnp.where(lane < 64, te, tw), pol_turn)
            crossed = roll_subs(jnp.where(lane < 64, tw, te), pol_turn)
            strip = jnp.where(is_polar, natural, roll_subs(pick(crossed, swap), 4))
            strip_old = roll_lanes(crossed, 64)
            halo = []
            halo_old = []
            for half in range(2):
                tile = 8 * (half * 4 + group)
                halo.append(
                    jnp.where(usecol[half], pick(pstar_ref[tile : tile + 8, :], index), strip)
                )
                tile = tile + 64
                halo_old.append(
                    jnp.where(usecol[half], pick(pstar_ref[tile : tile + 8, :], index), strip_old)
                )
            t2_halo = pick(corner[group], index)
            return cells, old, t2, t2_old, halo, halo_old, t2_halo

        tiles = [gather_tiles(v) for v in range(VARS)]
        u, w = tiles[0], tiles[1]
        cu_c = [cz[h] * u[0][h] for h in range(2)] + [zc_outer * u[2]]
        cv_c = [mc * w[0][h] for h in range(2)] + [mc * w[2]]
        cu_h = [cz[h] * u[4][h] for h in range(2)]
        cv_h = [mc * w[4][h] for h in range(2)]

        def tend(x, other, merid, cu, cv, s, m):
            zonal = ahead(x, other, s) - behind(x, other, s)
            second = ahead(x, other, m) + behind(x, other, m) - 2.0 * x
            return fc * second - cu * zonal - cv * merid

        fresh = []
        for v in range(VARS):
            cells, old, t2, t2_old, halo, halo_old, t2_halo = tiles[v]
            md = merid_of(cells[0], cells[1], t2, True)
            mh = merid_of(halo[0], halo[1], t2_halo, False)
            new = []
            new_halo = []
            filtered = []
            for h in range(2):
                x, o = cells[h], halo[h]
                n = old[h] + tend(x, o, md[h], cu_c[h], cv_c[h], s_tab[h], m_tab[h])
                new.append(n)
                filtered.append(x + 0.1 * (old[h] - 2.0 * x + n))
                new_halo.append(
                    halo_old[h] + tend(o, x, mh[h], cu_h[h], cv_h[h], s_tab[h], m_tab[h])
                )
            right = ahead(t2, t2_halo, one_tab)
            left = behind(t2, t2_halo, one_tab)
            new_t2 = t2_old + (
                fc * (right + left - 2.0 * t2) - cu_c[2] * (right - left) - cv_c[2] * md[2]
            )
            fresh.append((new, new_halo, new_t2, filtered))

        cu = [cz[h] * fresh[0][0][h] for h in range(2)]
        cv = [mc * fresh[1][0][h] for h in range(2)]
        for v in range(VARS):
            new, new_halo, new_t2, filtered = fresh[v]
            md = merid_of(new[0], new[1], new_t2, False)
            both = []
            for h in range(2):
                x = new[h]
                n = filtered[h] + tend(x, new_halo[h], md[h], cu[h], cv[h], s_tab[h], m_tab[h])
                outn_ref[v, k, 8 * h : 8 * h + 8, :] = n
                outp_ref[v, k, 8 * h : 8 * h + 8, :] = x + 0.1 * (filtered[h] - 2.0 * x + n)
                both.append(n)
            feats_ref[k, 16 * v : 16 * v + 16, :] = jnp.concatenate(both, axis=0).astype(bf16)
        pltpu.make_async_copy(outp_ref.at[:, k], prev_out.at[:, k], sems.at[k, 0]).start()
        pltpu.make_async_copy(outn_ref.at[0:2, k], now_out.at[0:2, k], sems.at[k, 1]).start()
        pltpu.make_async_copy(outn_ref.at[3:7, k], now_out.at[3:7, k], sems.at[k, 2]).start()
        return carry

    lax.fori_loop(0, LEV, level, 0)

    listed = listed_ref[...]
    live = lax.broadcasted_iota(jnp.int32, (1, LISTED), 1) < count_ref[0]
    row_hot = (listed // LANES == lax.broadcasted_iota(jnp.int32, (ROWS, LISTED), 0)) & live
    col_hot = listed % LANES == lax.broadcasted_iota(jnp.int32, (LANES, LISTED), 0)
    mask_ref[...] = lax.dot_general(
        jnp.where(row_hot, 1.0, 0.0).astype(bf16),
        jnp.where(col_hot, 1.0, 0.0).astype(bf16),
        (((1,), (1,)), ((), ())),
        preferred_element_type=f32,
    )

    column = lax.broadcasted_iota(jnp.int32, (HID, VARS * ROWS), 1) % ROWS
    start_sum = None
    for i in range(GPT // 8):
        t = jnp.exp2(-TAU_SCALE * start_ref[8 * i : 8 * i + 8, :])
        start_sum = t if start_sum is None else start_sum + t
    half_g = GPT // 2

    def network(r, carry):
        w1 = jnp.where(column == r, w1_ref[...], 0.0).astype(bf16)
        for k in range(LEV):
            z = jnp.dot(w1, feats_ref[k], preferred_element_type=f32) + b1_ref[...]
            h1_ref[k] = (z * jnp.tanh(z) + z).astype(bf16)
        for k in range(LEV):
            z = jnp.dot(w2_ref[...], h1_ref[k], preferred_element_type=f32) + b2_ref[...]
            h2_ref[k] = (z * jnp.tanh(z) + z).astype(bf16)
        for part in range(2):
            at = part * half_g
            total = start_ref[at : at + half_g, :]
            for k in range(LEV):
                y = jnp.dot(w3_ref[at : at + half_g, :], h2_ref[k], preferred_element_type=f32)
                y = y * LOG2E + b3_ref[at : at + half_g, :]
                e = jnp.exp2(jnp.minimum(y, 126.0))
                total = total + jnp.maximum(y, jnp.log2(1.0 + e))
                t = jnp.exp2(-TAU_SCALE * total)
                s = t[0:8]
                for i in range(1, half_g // 8):
                    s = s + t[8 * i : 8 * i + 8]
                if part == 0:
                    part_ref[k] = s
                else:
                    part_ref[k] = part_ref[k] + s
        lit = mask_ref[pl.ds(r, 1), :] > 0.5
        before = start_sum
        for k in range(LEV):
            after = part_ref[k]
            heat = jnp.sum(before - after, axis=0, keepdims=True)
            before = after
            outn_ref[2, k, pl.ds(r, 1), :] = outn_ref[2, k, pl.ds(r, 1), :] + jnp.where(
                lit, heat, 0.0
            )
        return carry

    lax.fori_loop(0, ROWS, network, 0)
    last = pltpu.make_async_copy(outn_ref.at[2], now_out.at[2], last_sem)
    last.start()

    def drain(k, carry):
        pltpu.make_async_copy(outp_ref.at[:, k], prev_out.at[:, k], sems.at[k, 0]).wait()
        pltpu.make_async_copy(outn_ref.at[0:2, k], now_out.at[0:2, k], sems.at[k, 1]).wait()
        pltpu.make_async_copy(outn_ref.at[3:7, k], now_out.at[3:7, k], sems.at[k, 2]).wait()
        return carry

    lax.fori_loop(0, LEV, drain, 0)
    last.wait()


VMEM = pl.BlockSpec(memory_space=pltpu.VMEM)
SMEM = pl.BlockSpec(memory_space=pltpu.SMEM)
ANY = pl.BlockSpec(memory_space=pl.ANY)


def body(
    state_prev,
    state_now,
    stride_table,
    filter_len,
    zonal_coef,
    merid_coef,
    filter_coef,
    w_first,
    b_first,
    w_second,
    b_second,
    w_third,
    b_third,
    band_weight,
    sunlit_cols,
    sunlit_count,
):
    first = (lax.axis_index("lat") == 0).astype(jnp.int32).reshape(1)
    zc = jnp.broadcast_to(zonal_coef[:, None], (ROWS, LANES))
    stride = jnp.broadcast_to(stride_table[:, None], (ROWS, LANES))
    flen = jnp.broadcast_to(filter_len[:, None], (ROWS, LANES))
    count = lax.dynamic_slice(sunlit_count.reshape(-1), (lax.axis_index("lon"),), (1,))

    lon_shape = jax.ShapeDtypeStruct((LON_ROWS, LANES), f32)
    lat_shape = jax.ShapeDtypeStruct((LAT_ROWS, LANES), f32)
    east, west, north, south = pl.pallas_call(
        pack_kernel,
        name="pack",
        out_shape=(lon_shape, lon_shape, lat_shape, lat_shape),
        in_specs=[SMEM, VMEM, VMEM, VMEM],
        out_specs=(VMEM,) * 4,
        compiler_params=pltpu.CompilerParams(vmem_limit_bytes=16 << 20),
    )(first, state_now, state_prev, zc)

    nlon = lax.axis_size("lon")
    nlat = lax.axis_size("lat")
    fromwest = lax.ppermute(east, "lon", [(i, (i + 1) % nlon) for i in range(nlon)])
    fromeast = lax.ppermute(west, "lon", [((i + 1) % nlon, i) for i in range(nlon)])

    east_cols = (jnp.arange(LANES) % 4 < 2)[None, :]

    def corners(half, row):
        at = col_tile(0, half, 0)
        pieces = [
            x[at : at + 32].reshape(4, 8, LANES)[:, row] for x in (fromeast, fromwest)
        ]
        return jnp.where(east_cols, pieces[0], pieces[1])

    north = lax.dynamic_update_slice(north, corners(0, 0), (LAT_ROWS - 8, 0))
    south = lax.dynamic_update_slice(south, corners(1, 7), (LAT_ROWS - 8, 0))
    fromnorth = lax.ppermute(south, "lat", [(i, i + 1) for i in range(nlat - 1)])
    fromsouth = lax.ppermute(north, "lat", [(i + 1, i) for i in range(nlat - 1)])

    def wide(vector):
        return jnp.broadcast_to(vector[:, None], (vector.shape[0], LANES))

    w1 = jnp.repeat(w_first.T.astype(f32) * 0.5, ROWS, axis=1)
    w2 = (w_second.T.astype(f32) * 0.5).astype(bf16)
    w3 = w_third.T
    b1 = wide(b_first * 0.5)
    b2 = wide(b_second * 0.5)
    b3 = wide(b_third * LOG2E)
    start = wide(jnp.log2(band_weight) * (-1.0 / TAU_SCALE))

    state = jax.ShapeDtypeStruct(state_now.shape, f32)
    prev_out, now_out = pl.pallas_call(
        main_kernel,
        name="main",
        out_shape=(state, state),
        in_specs=[SMEM] * 4 + [VMEM] * 17,
        out_specs=(ANY, ANY),
        scratch_shapes=[
            pltpu.VMEM(state_now.shape, f32),
            pltpu.VMEM(state_now.shape, f32),
            pltpu.VMEM((LEV, VARS * ROWS, LANES), bf16),
            pltpu.VMEM((8 * TILES_COLS, LANES), f32),
            pltpu.VMEM((LEV, HID, LANES), bf16),
            pltpu.VMEM((LEV, HID, LANES), bf16),
            pltpu.VMEM((LEV, 8, LANES), f32),
            pltpu.VMEM((ROWS, LANES), f32),
            pltpu.SemaphoreType.DMA((LEV, 3)),
            pltpu.SemaphoreType.DMA,
        ],
        compiler_params=pltpu.CompilerParams(vmem_limit_bytes=36 << 20),
    )(
        first,
        count,
        merid_coef,
        filter_coef,
        state_now,
        state_prev,
        fromwest,
        fromeast,
        fromnorth,
        fromsouth,
        stride,
        flen,
        zc,
        sunlit_cols.reshape(1, LISTED),
        w1,
        b1,
        w2,
        b2,
        w3,
        b3,
        start,
    )
    return prev_out, now_out


def solution(mesh):
    in_specs = (
        P(None, None, "lat", "lon"),
        P(None, None, "lat", "lon"),
        P("lat"),
        P("lat"),
        P("lat"),
        P(),
        P(),
        P(),
        P(),
        P(),
        P(),
        P(),
        P(),
        P(),
        P("lat", "lon", None),
        P("lat", None),
    )
    out_specs = (P(None, None, "lat", "lon"), P(None, None, "lat", "lon"))
    return jax.shard_map(body, mesh=mesh, in_specs=in_specs, out_specs=out_specs, check_vma=False)
```

```python
import functools

import jax
import jax.numpy as jnp
from jax import lax
from jax.experimental import pallas as pl
from jax.experimental.pallas import tpu as pltpu
from jax.sharding import PartitionSpec as P

VARS = 7
LEV = 16
ROWS = 16
LANES = 128
POLAR = 4
NETWORK = True
NLEVELS = 16
PARTS = ((0, 112), (112, 112))
HID = 64
GPT = 224
LISTED = 1536
TILES_POLAR = VARS * LEV // 2
TILES_COLS = 16
LON_ROWS = 8 * (TILES_POLAR + TILES_COLS)
LAT_NOW = VARS * 4
LAT_PREV = VARS * 2
LAT_ROWS = 8 * (LAT_NOW + LAT_PREV + 1)
LOG2E = 1.4426950408889634
TAU_SCALE = 0.15

f32 = jnp.float32
bf16 = jnp.bfloat16


def iotas():
    lane = lax.broadcasted_iota(jnp.int32, (8, LANES), 1)
    sub = lax.broadcasted_iota(jnp.int32, (8, LANES), 0)
    return lane, sub


def roll_lanes(x, shift):
    return pltpu.roll(x, shift, 1)


def roll_subs(x, shift):
    return pltpu.roll(x, shift, 0)


def pick(x, index):
    return jnp.take_along_axis(x, index, axis=1, mode="promise_in_bounds")


def col_tile(which, half, group):
    return 8 * (TILES_POLAR + which * 8 + half * 4 + group)


def pack_kernel(
    first_ref, zc_ref, now_hbm, prev_hbm, east_ref, west_ref, north_ref, south_ref, now_ref, prev_ref, sems
):
    def fetch(k, which):
        src, dst = ((now_hbm, now_ref), (prev_hbm, prev_ref))[which]
        return pltpu.make_async_copy(src.at[:, k], dst.at[:, k], sems.at[which, k])

    def start(k, carry):
        for part in range(2):
            for which in range(2):
                fetch(k + 8 * part, which).start()
        return carry

    lax.fori_loop(0, 8, start, 0)
    lane, sub = iotas()
    first = first_ref[0]
    base = pl.multiple_of(jnp.where(first == 1, 0, 8), 8)
    turn = jnp.where(first == 1, 0, 4)
    extra = jnp.where(first == 1, 4, 11)

    def levels(k, tiles):
        for part in range(2):
            for which in range(2):
                fetch(k + 8 * part, which).wait()
        for v in range(VARS):
            both = []
            for ref in (now_ref, prev_ref):
                pair = [
                    roll_subs(ref[v, k + 8 * part, pl.ds(base, 8), :], (4 * part + turn) % 8)
                    for part in range(2)
                ]
                both.append(jnp.where(sub < 4, pair[0], pair[1]))
            tile, old = both[0], roll_lanes(both[1], 64)
            row = jnp.where(
                sub < 4,
                jnp.broadcast_to(now_ref[v, k, pl.ds(extra, 1), :], (8, LANES)),
                jnp.broadcast_to(now_ref[v, k + 8, pl.ds(extra, 1), :], (8, LANES)),
            )
            at = pl.multiple_of((v * 8 + k) * 8, 8)
            east_ref[pl.ds(at, 8), :] = jnp.where(
                lane >= 64, tile, jnp.where(lane >= 32, old, roll_lanes(row, 32))
            )
            west_ref[pl.ds(at, 8), :] = jnp.where(
                lane < 64, tile, jnp.where(lane < 96, old, roll_lanes(row, 96))
            )
        tiles = list(tiles)
        for part in range(2):
            for v in range(VARS):
                at = (v % 2) * 64 + 4 * (k + 8 * part)
                mine = (lane >= at) & (lane < at + 4)
                for which, ref in enumerate((now_ref, prev_ref)):
                    for half in range(2):
                        x = ref[v, k + 8 * part, 8 * half : 8 * half + 8, :]
                        slot = which * 8 + half * 4 + v // 2
                        tiles[slot] = jnp.where(mine, roll_lanes(x, at + 2), tiles[slot])
        return tuple(tiles)

    tiles = lax.fori_loop(0, 8, levels, (jnp.zeros((8, LANES), f32),) * TILES_COLS)
    for i in range(TILES_COLS):
        at = 8 * (TILES_POLAR + i)
        west_ref[at : at + 8, :] = tiles[i]
        east_ref[at : at + 8, :] = tiles[i]

    def rows_now(g, carry):
        for v in range(VARS):
            north = None
            south = None
            for h in range(4):
                up = now_ref[v, g + 4 * h, 0:8, :]
                down = now_ref[v, g + 4 * h, 8:16, :]
                up = roll_subs(up, 2 * h) if h else up
                down = roll_subs(down, (2 * h + 2) % 8) if h != 3 else down
                mask = sub >= 2 * h
                north = up if h == 0 else jnp.where(mask, up, north)
                south = down if h == 0 else jnp.where(mask, down, south)
            at = pl.multiple_of((v * 4 + g) * 8, 8)
            north_ref[pl.ds(at, 8), :] = north
            south_ref[pl.ds(at, 8), :] = south
        return carry

    lax.fori_loop(0, 4, rows_now, 0)

    def rows_prev(g, carry):
        for v in range(VARS):
            north = None
            south = None
            for h in range(8):
                up = prev_ref[v, g + 2 * h, 0:8, :]
                down = prev_ref[v, g + 2 * h, 8:16, :]
                up = roll_subs(up, h) if h else up
                down = roll_subs(down, h + 1) if h != 7 else down
                mask = sub >= h
                north = up if h == 0 else jnp.where(mask, up, north)
                south = down if h == 0 else jnp.where(mask, down, south)
            at = pl.multiple_of((LAT_NOW + v * 2 + g) * 8, 8)
            north_ref[pl.ds(at, 8), :] = north
            south_ref[pl.ds(at, 8), :] = south
        return carry

    lax.fori_loop(0, 2, rows_prev, 0)
    north_ref[LAT_ROWS - 8 :, :] = jnp.full((8, LANES), zc_ref[0], f32)
    south_ref[LAT_ROWS - 8 :, :] = jnp.full((8, LANES), zc_ref[ROWS - 1], f32)


def prep_kernel(
    lon_ref,
    stride_ref,
    flen_ref,
    zc_ref,
    count_ref,
    listed_ref,
    w1_ref,
    shift_out,
    cz_out,
    mask_out,
    w1_out,
):
    sub = lax.broadcasted_iota(jnp.int32, (ROWS, LANES), 0)
    tables = []
    for ref in (stride_ref, flen_ref, zc_ref):
        x = jnp.full((ROWS, LANES), ref[0])
        for j in range(1, ROWS):
            x = jnp.where(sub == j, ref[j], x)
        tables.append(x)
    shift_out[0:ROWS, :] = tables[0]
    shift_out[ROWS : 2 * ROWS, :] = tables[1]
    cz_out[...] = tables[2] * (1.0 / tables[0].astype(f32))

    listed = listed_ref[...]
    live = lax.broadcasted_iota(jnp.int32, (1, LISTED), 1) < count_ref[0, lon_ref[0]]
    row_hot = (listed // LANES == lax.broadcasted_iota(jnp.int32, (ROWS, LISTED), 0)) & live
    col_hot = listed % LANES == lax.broadcasted_iota(jnp.int32, (LANES, LISTED), 0)
    mask_out[...] = lax.dot_general(
        jnp.where(row_hot, 1.0, 0.0).astype(bf16),
        jnp.where(col_hot, 1.0, 0.0).astype(bf16),
        (((1,), (1,)), ((), ())),
        preferred_element_type=f32,
    )
    column = lax.broadcasted_iota(jnp.int32, (HID, VARS * ROWS), 1) % ROWS
    w1 = w1_ref[...]
    for r in range(ROWS):
        w1_out[r] = jnp.where(column == r, w1, 0.0).astype(bf16)


def main_kernel(
    first_ref,
    merid_ref,
    filter_ref,
    now_ref,
    prev_ref,
    fromwest_ref,
    fromeast_ref,
    fromnorth_ref,
    fromsouth_ref,
    shift_ref,
    cz_ref,
    mask_ref,
    w1_ref,
    b1_ref,
    w2_ref,
    b2_ref,
    w3_ref,
    b3_ref,
    start_ref,
    prev_out,
    now_out,
    outp_ref,
    outn_ref,
    feats_ref,
    pstar_ref,
    h2a_ref,
    h2b_ref,
    part_ref,
    sems,
    last_sem,
):
    lane, sub = iotas()
    first = first_ref[0]
    west_cols = (lane % 4) < 2
    for i in range(TILES_COLS):
        at = 8 * (TILES_POLAR + i)
        pstar_ref[8 * i : 8 * i + 8, :] = jnp.where(
            west_cols, fromwest_ref[at : at + 8, :], fromeast_ref[at : at + 8, :]
        )

    def outer(at):
        return jnp.where(
            sub == 7,
            jnp.broadcast_to(fromnorth_ref[at : at + 1, :], (8, LANES)),
            jnp.broadcast_to(fromsouth_ref[at : at + 1, :], (8, LANES)),
        )

    edge = (lane < 2) | (lane >= 126)

    def shifts(amount):
        return (
            (lane + amount) % LANES,
            lane < amount,
            (lane - amount) % LANES,
            lane >= LANES - amount,
        )

    def around(x, other, tab):
        if tab is None:
            return (
                roll_lanes(jnp.where(lane == 0, other, x), LANES - 1),
                roll_lanes(jnp.where(lane == LANES - 1, other, x), 1),
            )
        return (
            pick(jnp.where(tab[1], other, x), tab[0]),
            pick(jnp.where(tab[3], other, x), tab[2]),
        )

    def merid_of(t0, t1, t2, last):
        u0, u1, u2 = (roll_subs(t, 7) for t in (t0, t1, t2))
        d0, d1, d2 = (roll_subs(t, 1) for t in (t0, t1, t2))
        bottom = sub == 7
        top = sub == 0
        out = [
            jnp.where(bottom, u1, u0) - jnp.where(top, d2, d0),
            jnp.where(bottom, u2, u1) - jnp.where(top, d0, d1),
        ]
        if last:
            out.append(jnp.where(bottom, u0, u2) - jnp.where(top, d1, d2))
        return out

    def take_steps(polar):
        is_polar = (sub < 4) if polar == 0 else (sub >= 4)

        def level(k, carry):
            mc = merid_ref[k]
            fc = filter_ref[k]
            pol_at = 8 * (k % 8)
            pol_turn = (4 * polar + 8 - 4 * (k // 8)) % 8
            gn, hn = k % 4, k // 4
            gp, hp = k % 2, k // 2
            s_tab = shifts(shift_ref[8 * polar : 8 * polar + 8, :])
            m_tab = shifts(shift_ref[ROWS + 8 * polar : ROWS + 8 * polar + 8, :])
            cz = [cz_ref[0:8, :], cz_ref[8:16, :], outer(LAT_ROWS - 4)]

            def gather_tiles(v):
                group = v // 2
                back = 126 - (v % 2) * 64 - 4 * k
                cells = [now_ref[v, k, 0:8, :], now_ref[v, k, 8:16, :]]
                old = [prev_ref[v, k, 0:8, :], prev_ref[v, k, 8:16, :]]
                at = pl.multiple_of((v * 4 + gn) * 8, 8)
                t2 = jnp.where(
                    sub >= 4,
                    roll_subs(fromnorth_ref[pl.ds(at, 8), :], (14 - 2 * hn) % 8),
                    roll_subs(fromsouth_ref[pl.ds(at, 8), :], (8 - 2 * hn) % 8),
                )
                at = pl.multiple_of((LAT_NOW + v * 2 + gp) * 8, 8)
                t2_old = jnp.where(
                    sub >= 4,
                    roll_subs(fromnorth_ref[pl.ds(at, 8), :], 7 - hp),
                    roll_subs(fromsouth_ref[pl.ds(at, 8), :], (8 - hp) % 8),
                )
                at = pl.multiple_of(v * 64 + pol_at, 8)
                te = fromeast_ref[pl.ds(at, 8), :]
                tw = fromwest_ref[pl.ds(at, 8), :]
                natural = roll_subs(jnp.where(lane < 64, te, tw), pol_turn)
                crossed = roll_subs(jnp.where(lane < 64, tw, te), pol_turn)
                near = jnp.where(lane < 64, roll_lanes(crossed, 32), roll_lanes(crossed, 96))
                strip = jnp.where(is_polar, natural, roll_subs(near, 4))
                strip_old = roll_lanes(crossed, 64)
                halo = []
                halo_old = []
                for half in range(2):
                    tile = 8 * (half * 4 + group)
                    x = roll_lanes(pstar_ref[tile : tile + 8, :], back)
                    halo.append(jnp.where(edge, x, strip) if half == polar else x)
                    x = roll_lanes(pstar_ref[tile + 64 : tile + 72, :], back)
                    halo_old.append(jnp.where(edge, x, strip_old) if half == polar else x)
                t2_halo = roll_lanes(outer(LAT_ROWS - 8 + group), back)
                return cells, old, t2, t2_old, halo, halo_old, t2_halo

            def tend(x, other, merid, cu, cv, half):
                right, left = around(x, other, s_tab if half == polar else None)
                zonal = right - left
                if half == polar:
                    right, left = around(x, other, m_tab)
                return fc * (right + left - 2.0 * x) - cu * zonal - cv * merid

            def first_step(tile, cu_c, cv_c, cu_h, cv_h):
                cells, old, t2, t2_old, halo, halo_old, t2_halo = tile
                md = merid_of(cells[0], cells[1], t2, True)
                mh = merid_of(halo[0], halo[1], t2_halo, False)
                new = []
                new_halo = []
                filtered = []
                for h in range(2):
                    x, o = cells[h], halo[h]
                    n = old[h] + tend(x, o, md[h], cu_c[h], cv_c[h], h)
                    new.append(n)
                    filtered.append(x + 0.1 * (old[h] - 2.0 * x + n))
                    new_halo.append(halo_old[h] + tend(o, x, mh[h], cu_h[h], cv_h[h], h))
                new_t2 = t2_old + tend(t2, t2_halo, md[2], cu_c[2], cv_c[2], 2)
                return new, new_halo, new_t2, filtered

            def second_step(v, stepped, cu, cv):
                new, new_halo, new_t2, filtered = stepped
                md = merid_of(new[0], new[1], new_t2, False)
                both = []
                for h in range(2):
                    x = new[h]
                    n = filtered[h] + tend(x, new_halo[h], md[h], cu[h], cv[h], h)
                    outn_ref[v, k, 8 * h : 8 * h + 8, :] = n
                    outp_ref[v, k, 8 * h : 8 * h + 8, :] = x + 0.1 * (filtered[h] - 2.0 * x + n)
                    both.append(n)
                at = pl.multiple_of((k % 2) * LANES, LANES)
                feats_ref[k // 2, 16 * v : 16 * v + 16, pl.ds(at, LANES)] = jnp.concatenate(
                    both, axis=0
                ).astype(bf16)

            u = gather_tiles(0)
            w = gather_tiles(1)
            cu_c = [cz[h] * u[0][h] for h in range(2)] + [cz[2] * u[2]]
            cv_c = [mc * w[0][h] for h in range(2)] + [mc * w[2]]
            cu_h = [cz[h] * u[4][h] for h in range(2)]
            cv_h = [mc * w[4][h] for h in range(2)]
            stepped_u = first_step(u, cu_c, cv_c, cu_h, cv_h)
            stepped_w = first_step(w, cu_c, cv_c, cu_h, cv_h)
            cu = [cz[h] * stepped_u[0][h] for h in range(2)]
            cv = [mc * stepped_w[0][h] for h in range(2)]
            second_step(0, stepped_u, cu, cv)
            second_step(1, stepped_w, cu, cv)
            for v in range(2, VARS):
                second_step(v, first_step(gather_tiles(v), cu_c, cv_c, cu_h, cv_h), cu, cv)
            pltpu.make_async_copy(outp_ref.at[:, k], prev_out.at[:, k], sems.at[k, 0]).start()
            pltpu.make_async_copy(outn_ref.at[0:2, k], now_out.at[0:2, k], sems.at[k, 1]).start()
            pltpu.make_async_copy(outn_ref.at[3:7, k], now_out.at[3:7, k], sems.at[k, 2]).start()
            return carry

        lax.fori_loop(0, NLEVELS, level, 0)

    @pl.when(first == 1)
    def _():
        take_steps(0)

    @pl.when(first != 1)
    def _():
        take_steps(1)

    start_sum = None
    for i in range(GPT // 8):
        t = jnp.exp2(-TAU_SCALE * start_ref[8 * i : 8 * i + 8, :])
        start_sum = t if start_sum is None else start_sum + t

    def hidden(r, p, dst):
        z = jnp.dot(w1_ref[r], feats_ref[p], preferred_element_type=f32)
        z = z + jnp.concatenate([b1_ref[...]] * 2, axis=1)
        h1 = (z * jnp.tanh(z) + z).astype(bf16)
        z = jnp.dot(w2_ref[...], h1, preferred_element_type=f32)
        z = z + jnp.concatenate([b2_ref[...]] * 2, axis=1)
        dst[p] = (z * jnp.tanh(z) + z).astype(bf16)

    def optics(at, width, p, src, total):
        y = jnp.dot(w3_ref[at : at + width, :], src[p], preferred_element_type=f32)
        for side in range(2):
            x = y[:, LANES * side : LANES * side + LANES] * LOG2E + b3_ref[at : at + width, :]
            e = jnp.exp2(jnp.minimum(x, 126.0))
            total = total + jnp.maximum(x, jnp.log2(1.0 + e))
            t = jnp.exp2(-TAU_SCALE * total)
            s = t[0:8]
            for i in range(1, width // 8):
                s = s + t[8 * i : 8 * i + 8]
            k = 2 * p + side
            part_ref[k] = s if at == 0 else part_ref[k] + s
        return total

    def phase(r, src, after, dst):
        done = 0
        turns = len(PARTS) * (LEV // 2)
        for n, (at, width) in enumerate(PARTS):
            total = start_ref[at : at + width, :]
            for p in range(LEV // 2):
                while done * turns < (LEV // 2) * (n * (LEV // 2) + p + 1):
                    hidden(after, done, dst)
                    done += 1
                total = optics(at, width, p, src, total)
        lit = mask_ref[pl.ds(r, 1), :] > 0.5
        before = start_sum
        for k in range(LEV):
            now = part_ref[k]
            heat = jnp.sum(before - now, axis=0, keepdims=True)
            before = now
            outn_ref[2, k, pl.ds(r, 1), :] = outn_ref[2, k, pl.ds(r, 1), :] + jnp.where(
                lit, heat, 0.0
            )

    def two_rows(i, carry):
        phase(2 * i, h2a_ref, 2 * i + 1, h2b_ref)
        phase(2 * i + 1, h2b_ref, jnp.minimum(2 * i + 2, ROWS - 1), h2a_ref)
        return carry

    for p in range(LEV // 2):
        hidden(0, p, h2a_ref)
    lax.fori_loop(0, ROWS // 2 if NETWORK else 0, two_rows, 0)
    last = pltpu.make_async_copy(outn_ref.at[2], now_out.at[2], last_sem)
    last.start()

    def drain(k, carry):
        pltpu.make_async_copy(outp_ref.at[:, k], prev_out.at[:, k], sems.at[k, 0]).wait()
        pltpu.make_async_copy(outn_ref.at[0:2, k], now_out.at[0:2, k], sems.at[k, 1]).wait()
        pltpu.make_async_copy(outn_ref.at[3:7, k], now_out.at[3:7, k], sems.at[k, 2]).wait()
        return carry

    lax.fori_loop(0, NLEVELS, drain, 0)
    last.wait()


VMEM = pl.BlockSpec(memory_space=pltpu.VMEM)
SMEM = pl.BlockSpec(memory_space=pltpu.SMEM)
ANY = pl.BlockSpec(memory_space=pl.ANY)
HBM = pl.BlockSpec(memory_space=pltpu.HBM)


def body(
    state_prev,
    state_now,
    stride_table,
    filter_len,
    zonal_coef,
    merid_coef,
    filter_coef,
    w_first,
    b_first,
    w_second,
    b_second,
    w_third,
    b_third,
    band_weight,
    sunlit_cols,
    sunlit_count,
):
    first = (lax.axis_index("lat") == 0).astype(jnp.int32).reshape(1)
    lon = lax.axis_index("lon").astype(jnp.int32).reshape(1)

    lon_shape = jax.ShapeDtypeStruct((LON_ROWS, LANES), f32)
    lat_shape = jax.ShapeDtypeStruct((LAT_ROWS, LANES), f32)
    state = jax.ShapeDtypeStruct(state_now.shape, f32)
    east, west, north, south = pl.pallas_call(
        pack_kernel,
        name="pack",
        out_shape=(lon_shape, lon_shape, lat_shape, lat_shape),
        in_specs=[SMEM, SMEM, HBM, HBM],
        out_specs=(VMEM,) * 4,
        scratch_shapes=[
            pltpu.VMEM(state_now.shape, f32),
            pltpu.VMEM(state_now.shape, f32),
            pltpu.SemaphoreType.DMA((2, LEV)),
        ],
        compiler_params=pltpu.CompilerParams(vmem_limit_bytes=16 << 20),
    )(first, zonal_coef, state_now, state_prev)

    def wide(vector):
        return jnp.broadcast_to(vector[:, None], (vector.shape[0], LANES))

    w1 = jnp.repeat(w_first.T.astype(f32) * 0.5, ROWS, axis=1)
    shift, cz, mask, w1 = pl.pallas_call(
        prep_kernel,
        name="prep",
        out_shape=(
            jax.ShapeDtypeStruct((2 * ROWS, LANES), jnp.int32),
            jax.ShapeDtypeStruct((ROWS, LANES), f32),
            jax.ShapeDtypeStruct((ROWS, LANES), f32),
            jax.ShapeDtypeStruct((ROWS, HID, VARS * ROWS), bf16),
        ),
        in_specs=[SMEM] * 5 + [VMEM] * 2,
        out_specs=(VMEM,) * 4,
        compiler_params=pltpu.CompilerParams(vmem_limit_bytes=8 << 20),
    )(lon, stride_table, filter_len, zonal_coef, sunlit_count, sunlit_cols.reshape(1, LISTED), w1)
    w2 = (w_second.T.astype(f32) * 0.5).astype(bf16)
    w3 = w_third.T
    b1 = wide(b_first * 0.5)
    b2 = wide(b_second * 0.5)
    b3 = wide(b_third * LOG2E)
    start = wide(jnp.log2(band_weight) * (-1.0 / TAU_SCALE))

    nlon = lax.axis_size("lon")
    nlat = lax.axis_size("lat")
    fromwest = lax.ppermute(east, "lon", [(i, (i + 1) % nlon) for i in range(nlon)])
    fromeast = lax.ppermute(west, "lon", [((i + 1) % nlon, i) for i in range(nlon)])

    west_cols = (jnp.arange(LANES) % 4 < 2)[None, :]

    def corners(half, row):
        at = col_tile(0, half, 0)
        pieces = [
            x[at : at + 32].reshape(4, 8, LANES)[:, row] for x in (fromwest, fromeast)
        ]
        return jnp.where(west_cols, pieces[0], pieces[1])

    north = lax.dynamic_update_slice(north, corners(0, 0), (LAT_ROWS - 8, 0))
    south = lax.dynamic_update_slice(south, corners(1, 7), (LAT_ROWS - 8, 0))
    (north, south, shift, cz, mask, w1, w2, w3, b1, b2, b3, start) = lax.optimization_barrier(
        (north, south, shift, cz, mask, w1, w2, w3, b1, b2, b3, start)
    )
    fromnorth = lax.ppermute(south, "lat", [(i, i + 1) for i in range(nlat - 1)])
    fromsouth = lax.ppermute(north, "lat", [(i + 1, i) for i in range(nlat - 1)])

    prev_out, now_out = pl.pallas_call(
        main_kernel,
        name="main",
        out_shape=(state, state),
        in_specs=[SMEM] * 3 + [VMEM] * 16,
        out_specs=(ANY, ANY),
        scratch_shapes=[
            pltpu.VMEM(state_now.shape, f32),
            pltpu.VMEM(state_now.shape, f32),
            pltpu.VMEM((LEV // 2, VARS * ROWS, 2 * LANES), bf16),
            pltpu.VMEM((8 * TILES_COLS, LANES), f32),
            pltpu.VMEM((LEV // 2, HID, 2 * LANES), bf16),
            pltpu.VMEM((LEV // 2, HID, 2 * LANES), bf16),
            pltpu.VMEM((LEV, 8, LANES), f32),
            pltpu.SemaphoreType.DMA((LEV, 3)),
            pltpu.SemaphoreType.DMA,
        ],
        compiler_params=pltpu.CompilerParams(vmem_limit_bytes=36 << 20),
    )(
        first,
        merid_coef,
        filter_coef,
        state_now,
        state_prev,
        fromwest,
        fromeast,
        fromnorth,
        fromsouth,
        shift,
        cz,
        mask,
        w1,
        b1,
        w2,
        b2,
        w3,
        b3,
        start,
    )
    return prev_out, now_out


def solution(mesh):
    in_specs = (
        P(None, None, "lat", "lon"),
        P(None, None, "lat", "lon"),
        P("lat"),
        P("lat"),
        P("lat"),
        P(),
        P(),
        P(),
        P(),
        P(),
        P(),
        P(),
        P(),
        P(),
        P("lat", "lon", None),
        P("lat", None),
    )
    out_specs = (P(None, None, "lat", "lon"), P(None, None, "lat", "lon"))
    return jax.shard_map(body, mesh=mesh, in_specs=in_specs, out_specs=out_specs, check_vma=False)
```

```python
import functools

import jax
import jax.numpy as jnp
from jax import lax
from jax.experimental import pallas as pl
from jax.experimental.pallas import tpu as pltpu
from jax.sharding import PartitionSpec as P

VARS = 7
LEV = 16
ROWS = 16
LANES = 128
POLAR = 4
NETWORK = True
STEPLIM = 8
MAINLIM = 16
NLEVELS = 16
PARTS = ((0, 112), (112, 112))
HID = 64
GPT = 224
LISTED = 1536
TILES_POLAR = VARS * LEV // 2
TILES_COLS = 16
LON_ROWS = 8 * (TILES_POLAR + TILES_COLS)
LAT_NOW = VARS * 4
LAT_PREV = VARS * 2
LAT_ROWS = 8 * (LAT_NOW + LAT_PREV + 1)
LOG2E = 1.4426950408889634
TAU_SCALE = 0.15

f32 = jnp.float32
bf16 = jnp.bfloat16


def iotas():
    lane = lax.broadcasted_iota(jnp.int32, (8, LANES), 1)
    sub = lax.broadcasted_iota(jnp.int32, (8, LANES), 0)
    return lane, sub


def roll_lanes(x, shift):
    return pltpu.roll(x, shift, 1)


def roll_subs(x, shift):
    return pltpu.roll(x, shift, 0)


def pick(x, index):
    return jnp.take_along_axis(x, index, axis=1, mode="promise_in_bounds")


def col_tile(which, half, group):
    return 8 * (TILES_POLAR + which * 8 + half * 4 + group)


def pack_kernel(
    first_ref,
    even_ref,
    zc_ref,
    now_hbm,
    prev_hbm,
    east_ref,
    west_ref,
    lata_ref,
    latb_ref,
    now_ref,
    prev_ref,
    sems,
):
    def fetch(k, which):
        src, dst = ((now_hbm, now_ref), (prev_hbm, prev_ref))[which]
        return pltpu.make_async_copy(src.at[:, k], dst.at[:, k], sems.at[which, k])

    def start(k, carry):
        for part in range(2):
            for which in range(2):
                fetch(k + 8 * part, which).start()
        return carry

    lax.fori_loop(0, 8, start, 0)
    lane, sub = iotas()
    first = first_ref[0]
    even = even_ref[0] == 1

    def put(at, north, south):
        lata_ref[pl.ds(at, 8), :] = jnp.where(even, south, north)
        latb_ref[pl.ds(at, 8), :] = jnp.where(even, north, south)

    base = pl.multiple_of(jnp.where(first == 1, 0, 8), 8)
    turn = jnp.where(first == 1, 0, 4)
    extra = jnp.where(first == 1, 4, 11)

    def levels(k, tiles):
        for part in range(2):
            for which in range(2):
                fetch(k + 8 * part, which).wait()
        for v in range(VARS):
            both = []
            for ref in (now_ref, prev_ref):
                pair = [
                    roll_subs(ref[v, k + 8 * part, pl.ds(base, 8), :], (4 * part + turn) % 8)
                    for part in range(2)
                ]
                both.append(jnp.where(sub < 4, pair[0], pair[1]))
            tile, old = both[0], roll_lanes(both[1], 64)
            row = jnp.where(
                sub < 4,
                jnp.broadcast_to(now_ref[v, k, pl.ds(extra, 1), :], (8, LANES)),
                jnp.broadcast_to(now_ref[v, k + 8, pl.ds(extra, 1), :], (8, LANES)),
            )
            at = pl.multiple_of((v * 8 + k) * 8, 8)
            east_ref[pl.ds(at, 8), :] = jnp.where(
                lane >= 64, tile, jnp.where(lane >= 32, old, roll_lanes(row, 32))
            )
            west_ref[pl.ds(at, 8), :] = jnp.where(
                lane < 64, tile, jnp.where(lane < 96, old, roll_lanes(row, 96))
            )
        tiles = list(tiles)
        for part in range(2):
            for v in range(VARS):
                at = (v % 2) * 64 + 4 * (k + 8 * part)
                mine = (lane >= at) & (lane < at + 4)
                for which, ref in enumerate((now_ref, prev_ref)):
                    for half in range(2):
                        x = ref[v, k + 8 * part, 8 * half : 8 * half + 8, :]
                        slot = which * 8 + half * 4 + v // 2
                        tiles[slot] = jnp.where(mine, roll_lanes(x, at + 2), tiles[slot])
        return tuple(tiles)

    tiles = lax.fori_loop(0, 8, levels, (jnp.zeros((8, LANES), f32),) * TILES_COLS)
    for i in range(TILES_COLS):
        at = 8 * (TILES_POLAR + i)
        west_ref[at : at + 8, :] = tiles[i]
        east_ref[at : at + 8, :] = tiles[i]

    def rows_now(g, carry):
        for v in range(VARS):
            north = None
            south = None
            for h in range(4):
                up = now_ref[v, g + 4 * h, 0:8, :]
                down = now_ref[v, g + 4 * h, 8:16, :]
                up = roll_subs(up, 2 * h) if h else up
                down = roll_subs(down, (2 * h + 2) % 8) if h != 3 else down
                mask = sub >= 2 * h
                north = up if h == 0 else jnp.where(mask, up, north)
                south = down if h == 0 else jnp.where(mask, down, south)
            at = pl.multiple_of((v * 4 + g) * 8, 8)
            put(at, north, south)
        return carry

    lax.fori_loop(0, 4, rows_now, 0)

    def rows_prev(g, carry):
        for v in range(VARS):
            north = None
            south = None
            for h in range(8):
                up = prev_ref[v, g + 2 * h, 0:8, :]
                down = prev_ref[v, g + 2 * h, 8:16, :]
                up = roll_subs(up, h) if h else up
                down = roll_subs(down, h + 1) if h != 7 else down
                mask = sub >= h
                north = up if h == 0 else jnp.where(mask, up, north)
                south = down if h == 0 else jnp.where(mask, down, south)
            at = pl.multiple_of((LAT_NOW + v * 2 + g) * 8, 8)
            put(at, north, south)
        return carry

    lax.fori_loop(0, 2, rows_prev, 0)
    put(
        LAT_ROWS - 8,
        jnp.full((8, LANES), zc_ref[0], f32),
        jnp.full((8, LANES), zc_ref[ROWS - 1], f32),
    )


def prep_kernel(
    lon_ref,
    stride_ref,
    flen_ref,
    zc_ref,
    count_ref,
    listed_ref,
    w1_ref,
    shift_out,
    cz_out,
    mask_out,
    w1_out,
):
    sub = lax.broadcasted_iota(jnp.int32, (ROWS, LANES), 0)
    tables = []
    for ref in (stride_ref, flen_ref, zc_ref):
        x = jnp.full((ROWS, LANES), ref[0])
        for j in range(1, ROWS):
            x = jnp.where(sub == j, ref[j], x)
        tables.append(x)
    shift_out[0:ROWS, :] = tables[0]
    shift_out[ROWS : 2 * ROWS, :] = tables[1]
    cz_out[...] = tables[2] * (1.0 / tables[0].astype(f32))

    listed = listed_ref[...]
    live = lax.broadcasted_iota(jnp.int32, (1, LISTED), 1) < count_ref[0, lon_ref[0]]
    row_hot = (listed // LANES == lax.broadcasted_iota(jnp.int32, (ROWS, LISTED), 0)) & live
    col_hot = listed % LANES == lax.broadcasted_iota(jnp.int32, (LANES, LISTED), 0)
    mask_out[...] = lax.dot_general(
        jnp.where(row_hot, 1.0, 0.0).astype(bf16),
        jnp.where(col_hot, 1.0, 0.0).astype(bf16),
        (((1,), (1,)), ((), ())),
        preferred_element_type=f32,
    )
    column = lax.broadcasted_iota(jnp.int32, (HID, VARS * ROWS), 1) % ROWS
    w1 = w1_ref[...]
    for r in range(ROWS):
        w1_out[r] = jnp.where(column == r, w1, 0.0).astype(bf16)


def shifts(amount):
    lane, _ = iotas()
    return (
        (lane + amount) % LANES,
        lane < amount,
        (lane - amount) % LANES,
        lane >= LANES - amount,
    )


def around(x, other, tab):
    lane, _ = iotas()
    if tab is None:
        return (
            roll_lanes(jnp.where(lane == 0, other, x), LANES - 1),
            roll_lanes(jnp.where(lane == LANES - 1, other, x), 1),
        )
    return (
        pick(jnp.where(tab[1], other, x), tab[0]),
        pick(jnp.where(tab[3], other, x), tab[2]),
    )


def merid_of(t0, t1, above, below):
    _, sub = iotas()
    u0, u1, d0, d1 = roll_subs(t0, 7), roll_subs(t1, 7), roll_subs(t0, 1), roll_subs(t1, 1)
    bottom = sub == 7
    top = sub == 0
    return (
        jnp.where(bottom, u1, u0) - jnp.where(top, above, d0),
        jnp.where(bottom, below, u1) - jnp.where(top, d0, d1),
    )


def tend(x, other, merid, cu, cv, fc, s_tab, m_tab):
    right, left = around(x, other, s_tab)
    zonal = right - left
    if m_tab is not None:
        right, left = around(x, other, m_tab)
    return fc * (right + left - 2.0 * x) - cu * zonal - cv * merid


def tables_of(shift_ref, polar):
    s_tab = shifts(shift_ref[8 * polar : 8 * polar + 8, :])
    m_tab = shifts(shift_ref[ROWS + 8 * polar : ROWS + 8 * polar + 8, :])
    return [(s_tab, m_tab) if h == polar else (None, None) for h in range(2)]


def step_kernel(
    first_ref,
    merid_ref,
    filter_ref,
    now_ref,
    prev_ref,
    fromwest_ref,
    fromeast_ref,
    shift_ref,
    cz_ref,
    new_ref,
    halo_ref,
    filtered_ref,
    wind_ref,
    pstar_ref,
):
    lane, sub = iotas()
    first = first_ref[0]
    west_cols = (lane % 4) < 2
    for i in range(TILES_COLS):
        at = 8 * (TILES_POLAR + i)
        pstar_ref[8 * i : 8 * i + 8, :] = jnp.where(
            west_cols, fromwest_ref[at : at + 8, :], fromeast_ref[at : at + 8, :]
        )
    edge = (lane < 2) | (lane >= 126)
    zero = jnp.zeros((8, LANES), f32)

    def take_step(polar):
        is_polar = (sub < 4) if polar == 0 else (sub >= 4)

        def level(k, carry):
            mc = merid_ref[k]
            fc = filter_ref[k]
            pol_at = 8 * (k % 8)
            pol_turn = (4 * polar + 8 - 4 * (k // 8)) % 8
            tabs = tables_of(shift_ref, polar)
            cz = [cz_ref[0:8, :], cz_ref[8:16, :]]

            def gather_tiles(v):
                group = v // 2
                back = 126 - (v % 2) * 64 - 4 * k
                cells = [now_ref[v, k, 0:8, :], now_ref[v, k, 8:16, :]]
                old = [prev_ref[v, k, 0:8, :], prev_ref[v, k, 8:16, :]]
                at = pl.multiple_of(v * 64 + pol_at, 8)
                te = fromeast_ref[pl.ds(at, 8), :]
                tw = fromwest_ref[pl.ds(at, 8), :]
                natural = roll_subs(jnp.where(lane < 64, te, tw), pol_turn)
                crossed = roll_subs(jnp.where(lane < 64, tw, te), pol_turn)
                near = jnp.where(lane < 64, roll_lanes(crossed, 32), roll_lanes(crossed, 96))
                strip = jnp.where(is_polar, natural, roll_subs(near, 4))
                strip_old = roll_lanes(crossed, 64)
                halo = []
                halo_old = []
                for half in range(2):
                    tile = 8 * (half * 4 + group)
                    x = roll_lanes(pstar_ref[tile : tile + 8, :], back)
                    halo.append(jnp.where(edge, x, strip) if half == polar else x)
                    x = roll_lanes(pstar_ref[tile + 64 : tile + 72, :], back)
                    halo_old.append(jnp.where(edge, x, strip_old) if half == polar else x)
                return cells, old, halo, halo_old

            def advance(v, tiles, cu_c, cv_c, cu_h, cv_h):
                cells, old, halo, halo_old = tiles
                md = merid_of(cells[0], cells[1], zero, zero)
                mh = merid_of(halo[0], halo[1], zero, zero)
                for h in range(2):
                    x, o = cells[h], halo[h]
                    rows = slice(8 * h, 8 * h + 8)
                    n = old[h] + tend(x, o, md[h], cu_c[h], cv_c[h], fc, *tabs[h])
                    new_ref[v, k, rows, :] = n
                    filtered_ref[v, k, rows, :] = x + 0.1 * (old[h] - 2.0 * x + n)
                    halo_ref[v, k, rows, :] = halo_old[h] + tend(
                        o, x, mh[h], cu_h[h], cv_h[h], fc, *tabs[h]
                    )

            u = gather_tiles(0)
            w = gather_tiles(1)
            cu_c = [cz[h] * u[0][h] for h in range(2)]
            cv_c = [mc * w[0][h] for h in range(2)]
            cu_h = [cz[h] * u[2][h] for h in range(2)]
            cv_h = [mc * w[2][h] for h in range(2)]
            for h in range(2):
                wind_ref[k, 8 * h : 8 * h + 8, :] = w[2][h]
            for v in range(VARS):
                tiles = u if v == 0 else w if v == 1 else gather_tiles(v)
                advance(v, tiles, cu_c, cv_c, cu_h, cv_h)
            return carry

        lax.fori_loop(0, LEV, level, 0)

    @pl.when(first == 1)
    def _():
        take_step(0)

    @pl.when(first != 1)
    def _():
        take_step(1)


def main_kernel(
    first_ref,
    even_ref,
    merid_ref,
    filter_ref,
    now_ref,
    new_ref,
    halo_ref,
    filtered_ref,
    wind_ref,
    froma_ref,
    fromb_ref,
    shift_ref,
    cz_ref,
    mask_ref,
    w1_ref,
    b1_ref,
    w2_ref,
    b2_ref,
    w3_ref,
    b3_ref,
    start_ref,
    prev_out,
    now_out,
    outp_ref,
    outn_ref,
    feats_ref,
    h2a_ref,
    h2b_ref,
    part_ref,
    sems,
    last_sem,
):
    lane, sub = iotas()
    first = first_ref[0]
    even = even_ref[0] == 1
    bottom = sub == 7
    top = sub == 0
    zero = jnp.zeros((8, LANES), f32)
    north_half = jnp.where(even, sub, 7 - sub) >= 4

    def outer(at):
        a = jnp.broadcast_to(froma_ref[at : at + 1, :], (8, LANES))
        b = jnp.broadcast_to(fromb_ref[at : at + 1, :], (8, LANES))
        return jnp.where(jnp.where(sub == 7, even_ref[0], 1 - even_ref[0]) == 1, b, a)

    def take_steps(polar):
        def level(k, carry):
            mc = merid_ref[k]
            fc = filter_ref[k]
            gn, hn = k % 4, k // 4
            gp, hp = k % 2, k // 2
            tabs = tables_of(shift_ref, polar)
            cz = [cz_ref[0:8, :], cz_ref[8:16, :], outer(LAT_ROWS - 4)]
            up_now, down_now = (14 - 2 * hn) % 8, (8 - 2 * hn) % 8
            up_old, down_old = 7 - hp, (8 - hp) % 8
            turn_now = (jnp.where(even, down_now, up_now), jnp.where(even, up_now, down_now))
            turn_old = (jnp.where(even, down_old, up_old), jnp.where(even, up_old, down_old))

            def outer_tiles(v):
                back = 126 - (v % 2) * 64 - 4 * k
                pair = []
                for at, turn in (
                    ((v * 4 + gn) * 8, turn_now),
                    ((LAT_NOW + v * 2 + gp) * 8, turn_old),
                ):
                    at = pl.multiple_of(at, 8)
                    a = roll_subs(froma_ref[pl.ds(at, 8), :], turn[0])
                    b = roll_subs(fromb_ref[pl.ds(at, 8), :], turn[1])
                    pair.append(jnp.where(north_half, b, a))
                return pair[0], pair[1], roll_lanes(outer(LAT_ROWS - 8 + v // 2), back)

            def first_step(v, tiles, cu_2, cv_2, cv_c, cv_h):
                t2, t2_old, t2_halo = tiles
                above = jnp.where(top, roll_subs(t2, 1), zero)
                below = jnp.where(bottom, roll_subs(t2, 7), zero)
                above_h = jnp.where(top, roll_subs(t2_halo, 1), zero)
                below_h = jnp.where(bottom, roll_subs(t2_halo, 7), zero)
                more = [cv_c[0] * above, -(cv_c[1] * below)]
                more_h = [cv_h[0] * above_h, -(cv_h[1] * below_h)]
                new = []
                new_halo = []
                filtered = []
                for h in range(2):
                    rows = slice(8 * h, 8 * h + 8)
                    new.append(new_ref[v, k, rows, :] + more[h])
                    filtered.append(filtered_ref[v, k, rows, :] + 0.1 * more[h])
                    new_halo.append(halo_ref[v, k, rows, :] + more_h[h])
                merid = jnp.where(
                    bottom, roll_subs(now_ref[v, k, 0:8, :], 7), roll_subs(t2, 7)
                ) - jnp.where(top, roll_subs(now_ref[v, k, 8:16, :], 1), roll_subs(t2, 1))
                new_t2 = t2_old + tend(t2, t2_halo, merid, cu_2, cv_2, fc, None, None)
                return new, new_halo, new_t2, filtered

            def second_step(v, stepped, cu, cv):
                new, new_halo, new_t2, filtered = stepped
                md = merid_of(new[0], new[1], roll_subs(new_t2, 1), roll_subs(new_t2, 7))
                both = []
                for h in range(2):
                    x = new[h]
                    n = filtered[h] + tend(x, new_halo[h], md[h], cu[h], cv[h], fc, *tabs[h])
                    outn_ref[v, k, 8 * h : 8 * h + 8, :] = n
                    outp_ref[v, k, 8 * h : 8 * h + 8, :] = x + 0.1 * (filtered[h] - 2.0 * x + n)
                    both.append(n)
                at = pl.multiple_of((k % 2) * LANES, LANES)
                feats_ref[k // 2, 16 * v : 16 * v + 16, pl.ds(at, LANES)] = jnp.concatenate(
                    both, axis=0
                ).astype(bf16)

            u = outer_tiles(0)
            w = outer_tiles(1)
            cu_2 = cz[2] * u[0]
            cv_2 = mc * w[0]
            cv_c = [mc * now_ref[1, k, 8 * h : 8 * h + 8, :] for h in range(2)]
            cv_h = [mc * wind_ref[k, 8 * h : 8 * h + 8, :] for h in range(2)]
            stepped_u = first_step(0, u, cu_2, cv_2, cv_c, cv_h)
            stepped_w = first_step(1, w, cu_2, cv_2, cv_c, cv_h)
            cu = [cz[h] * stepped_u[0][h] for h in range(2)]
            cv = [mc * stepped_w[0][h] for h in range(2)]
            second_step(0, stepped_u, cu, cv)
            second_step(1, stepped_w, cu, cv)
            for v in range(2, VARS):
                second_step(v, first_step(v, outer_tiles(v), cu_2, cv_2, cv_c, cv_h), cu, cv)
            pltpu.make_async_copy(outp_ref.at[:, k], prev_out.at[:, k], sems.at[k, 0]).start()
            pltpu.make_async_copy(outn_ref.at[0:2, k], now_out.at[0:2, k], sems.at[k, 1]).start()
            pltpu.make_async_copy(outn_ref.at[3:7, k], now_out.at[3:7, k], sems.at[k, 2]).start()
            return carry

        lax.fori_loop(0, NLEVELS, level, 0)

    @pl.when(first == 1)
    def _():
        take_steps(0)

    @pl.when(first != 1)
    def _():
        take_steps(1)

    start_sum = None
    for i in range(GPT // 8):
        t = jnp.exp2(-TAU_SCALE * start_ref[8 * i : 8 * i + 8, :])
        start_sum = t if start_sum is None else start_sum + t

    def hidden(r, p, dst):
        z = jnp.dot(w1_ref[r], feats_ref[p], preferred_element_type=f32)
        z = z + jnp.concatenate([b1_ref[...]] * 2, axis=1)
        h1 = (z * jnp.tanh(z) + z).astype(bf16)
        z = jnp.dot(w2_ref[...], h1, preferred_element_type=f32)
        z = z + jnp.concatenate([b2_ref[...]] * 2, axis=1)
        dst[p] = (z * jnp.tanh(z) + z).astype(bf16)

    def optics(at, width, p, src, total):
        y = jnp.dot(w3_ref[at : at + width, :], src[p], preferred_element_type=f32)
        for side in range(2):
            x = y[:, LANES * side : LANES * side + LANES] * LOG2E + b3_ref[at : at + width, :]
            e = jnp.exp2(jnp.minimum(x, 126.0))
            total = total + jnp.maximum(x, jnp.log2(1.0 + e))
            t = jnp.exp2(-TAU_SCALE * total)
            s = t[0:8]
            for i in range(1, width // 8):
                s = s + t[8 * i : 8 * i + 8]
            k = 2 * p + side
            part_ref[k] = s if at == 0 else part_ref[k] + s
        return total

    def phase(r, src, after, dst):
        done = 0
        turns = len(PARTS) * (LEV // 2)
        for n, (at, width) in enumerate(PARTS):
            total = start_ref[at : at + width, :]
            for p in range(LEV // 2):
                while done * turns < (LEV // 2) * (n * (LEV // 2) + p + 1):
                    hidden(after, done, dst)
                    done += 1
                total = optics(at, width, p, src, total)
        lit = mask_ref[pl.ds(r, 1), :] > 0.5
        before = start_sum
        for k in range(LEV):
            now = part_ref[k]
            heat = jnp.sum(before - now, axis=0, keepdims=True)
            before = now
            outn_ref[2, k, pl.ds(r, 1), :] = outn_ref[2, k, pl.ds(r, 1), :] + jnp.where(
                lit, heat, 0.0
            )

    def two_rows(i, carry):
        phase(2 * i, h2a_ref, 2 * i + 1, h2b_ref)
        phase(2 * i + 1, h2b_ref, jnp.minimum(2 * i + 2, ROWS - 1), h2a_ref)
        return carry

    for p in range(LEV // 2):
        hidden(0, p, h2a_ref)
    lax.fori_loop(0, ROWS // 2 if NETWORK else 0, two_rows, 0)
    last = pltpu.make_async_copy(outn_ref.at[2], now_out.at[2], last_sem)
    last.start()

    def drain(k, carry):
        pltpu.make_async_copy(outp_ref.at[:, k], prev_out.at[:, k], sems.at[k, 0]).wait()
        pltpu.make_async_copy(outn_ref.at[0:2, k], now_out.at[0:2, k], sems.at[k, 1]).wait()
        pltpu.make_async_copy(outn_ref.at[3:7, k], now_out.at[3:7, k], sems.at[k, 2]).wait()
        return carry

    lax.fori_loop(0, NLEVELS, drain, 0)
    last.wait()


VMEM = pl.BlockSpec(memory_space=pltpu.VMEM)
SMEM = pl.BlockSpec(memory_space=pltpu.SMEM)
ANY = pl.BlockSpec(memory_space=pl.ANY)
HBM = pl.BlockSpec(memory_space=pltpu.HBM)


def body(
    state_prev,
    state_now,
    stride_table,
    filter_len,
    zonal_coef,
    merid_coef,
    filter_coef,
    w_first,
    b_first,
    w_second,
    b_second,
    w_third,
    b_third,
    band_weight,
    sunlit_cols,
    sunlit_count,
):
    first = (lax.axis_index("lat") == 0).astype(jnp.int32).reshape(1)
    even = (lax.axis_index("lat") % 2 == 0).astype(jnp.int32).reshape(1)
    lon = lax.axis_index("lon").astype(jnp.int32).reshape(1)

    lon_shape = jax.ShapeDtypeStruct((LON_ROWS, LANES), f32)
    lat_shape = jax.ShapeDtypeStruct((LAT_ROWS, LANES), f32)
    state = jax.ShapeDtypeStruct(state_now.shape, f32)
    east, west, lata, latb = pl.pallas_call(
        pack_kernel,
        name="pack",
        out_shape=(lon_shape, lon_shape, lat_shape, lat_shape),
        in_specs=[SMEM, SMEM, SMEM, HBM, HBM],
        out_specs=(VMEM,) * 4,
        scratch_shapes=[
            pltpu.VMEM(state_now.shape, f32),
            pltpu.VMEM(state_now.shape, f32),
            pltpu.SemaphoreType.DMA((2, LEV)),
        ],
        compiler_params=pltpu.CompilerParams(vmem_limit_bytes=16 << 20),
    )(first, even, zonal_coef, state_now, state_prev)

    def wide(vector):
        return jnp.broadcast_to(vector[:, None], (vector.shape[0], LANES))

    w1 = jnp.repeat(w_first.T.astype(f32) * 0.5, ROWS, axis=1)
    shift, cz, mask, w1 = pl.pallas_call(
        prep_kernel,
        name="prep",
        out_shape=(
            jax.ShapeDtypeStruct((2 * ROWS, LANES), jnp.int32),
            jax.ShapeDtypeStruct((ROWS, LANES), f32),
            jax.ShapeDtypeStruct((ROWS, LANES), f32),
            jax.ShapeDtypeStruct((ROWS, HID, VARS * ROWS), bf16),
        ),
        in_specs=[SMEM] * 5 + [VMEM] * 2,
        out_specs=(VMEM,) * 4,
        compiler_params=pltpu.CompilerParams(vmem_limit_bytes=8 << 20),
    )(lon, stride_table, filter_len, zonal_coef, sunlit_count, sunlit_cols.reshape(1, LISTED), w1)
    w2 = (w_second.T.astype(f32) * 0.5).astype(bf16)
    w3 = w_third.T
    b1 = wide(b_first * 0.5)
    b2 = wide(b_second * 0.5)
    b3 = wide(b_third * LOG2E)
    start = wide(jnp.log2(band_weight) * (-1.0 / TAU_SCALE))

    nlon = lax.axis_size("lon")
    nlat = lax.axis_size("lat")
    fromwest = lax.ppermute(east, "lon", [(i, (i + 1) % nlon) for i in range(nlon)])
    fromeast = lax.ppermute(west, "lon", [((i + 1) % nlon, i) for i in range(nlon)])

    west_cols = (jnp.arange(LANES) % 4 < 2)[None, :]

    def corners(half, row):
        at = col_tile(0, half, 0)
        pieces = [
            x[at : at + 32].reshape(4, 8, LANES)[:, row] for x in (fromwest, fromeast)
        ]
        return jnp.where(west_cols, pieces[0], pieces[1])

    north, south = corners(0, 0), corners(1, 7)
    lata = lax.dynamic_update_slice(lata, jnp.where(even == 1, south, north), (LAT_ROWS - 8, 0))
    latb = lax.dynamic_update_slice(latb, jnp.where(even == 1, north, south), (LAT_ROWS - 8, 0))
    (lata, latb, shift, cz, mask, w1, w2, w3, b1, b2, b3, start) = lax.optimization_barrier(
        (lata, latb, shift, cz, mask, w1, w2, w3, b1, b2, b3, start)
    )
    swap_a = [(i, i ^ 1) for i in range(nlat)]
    swap_b = [(i, i + 1 if i % 2 else i - 1) for i in range(1, nlat - 1)]
    froma = lax.ppermute(lata, "lat", swap_a)
    fromb = lax.ppermute(latb, "lat", swap_b)

    new, halo, filtered, wind = pl.pallas_call(
        step_kernel,
        name="step",
        out_shape=(state, state, state, jax.ShapeDtypeStruct((LEV, ROWS, LANES), f32)),
        in_specs=[SMEM] * 3 + [VMEM] * 6,
        out_specs=(VMEM,) * 4,
        scratch_shapes=[pltpu.VMEM((8 * TILES_COLS, LANES), f32)],
        cost_estimate=pl.CostEstimate(
            flops=20_000_000, bytes_accessed=24_000_000, transcendentals=0
        ),
        compiler_params=pltpu.CompilerParams(vmem_limit_bytes=STEPLIM << 20),
    )(
        first,
        merid_coef,
        filter_coef,
        state_now,
        state_prev,
        fromwest,
        fromeast,
        shift,
        cz,
    )

    prev_out, now_out = pl.pallas_call(
        main_kernel,
        name="main",
        out_shape=(state, state),
        in_specs=[SMEM] * 4 + [VMEM] * 17,
        out_specs=(ANY, ANY),
        scratch_shapes=[
            pltpu.VMEM(state_now.shape, f32),
            pltpu.VMEM(state_now.shape, f32),
            pltpu.VMEM((LEV // 2, VARS * ROWS, 2 * LANES), bf16),
            pltpu.VMEM((LEV // 2, HID, 2 * LANES), bf16),
            pltpu.VMEM((LEV // 2, HID, 2 * LANES), bf16),
            pltpu.VMEM((LEV, 8, LANES), f32),
            pltpu.SemaphoreType.DMA((LEV, 3)),
            pltpu.SemaphoreType.DMA,
        ],
        compiler_params=pltpu.CompilerParams(vmem_limit_bytes=MAINLIM << 20),
    )(
        first,
        even,
        merid_coef,
        filter_coef,
        state_now,
        new,
        halo,
        filtered,
        wind,
        froma,
        fromb,
        shift,
        cz,
        mask,
        w1,
        b1,
        w2,
        b2,
        w3,
        b3,
        start,
    )
    return prev_out, now_out


def solution(mesh):
    in_specs = (
        P(None, None, "lat", "lon"),
        P(None, None, "lat", "lon"),
        P("lat"),
        P("lat"),
        P("lat"),
        P(),
        P(),
        P(),
        P(),
        P(),
        P(),
        P(),
        P(),
        P(),
        P("lat", "lon", None),
        P("lat", None),
    )
    out_specs = (P(None, None, "lat", "lon"), P(None, None, "lat", "lon"))
    return jax.shard_map(body, mesh=mesh, in_specs=in_specs, out_specs=out_specs, check_vma=False)
```

```python
import functools

import jax
import jax.numpy as jnp
from jax import lax
from jax.experimental import pallas as pl
from jax.experimental.pallas import tpu as pltpu
from jax.sharding import PartitionSpec as P

VARS = 7
LEV = 16
ROWS = 16
LANES = 128
POLAR = 4
NETWORK = True
STEPLIM = 8
MAINLIM = 16
NLEVELS = 16
PARTS = ((0, 112), (112, 112))
HID = 64
GPT = 224
LISTED = 1536
TILES_POLAR = VARS * LEV // 2
TILES_COLS = 16
LON_ROWS = 8 * (TILES_POLAR + TILES_COLS)
LAT_NOW = VARS * 4
LAT_PREV = VARS * 2
LAT_ROWS = 8 * (LAT_NOW + LAT_PREV + 1)
LOG2E = 1.4426950408889634
TAU_SCALE = 0.15

f32 = jnp.float32
bf16 = jnp.bfloat16


def iotas():
    lane = lax.broadcasted_iota(jnp.int32, (8, LANES), 1)
    sub = lax.broadcasted_iota(jnp.int32, (8, LANES), 0)
    return lane, sub


def roll_lanes(x, shift):
    return pltpu.roll(x, shift, 1)


def roll_subs(x, shift):
    return pltpu.roll(x, shift, 0)


def pick(x, index):
    return jnp.take_along_axis(x, index, axis=1, mode="promise_in_bounds")


def col_tile(which, half, group):
    return 8 * (TILES_POLAR + which * 8 + half * 4 + group)


def pack_kernel(
    first_ref,
    even_ref,
    now_hbm,
    prev_hbm,
    east_ref,
    west_ref,
    lata_ref,
    latb_ref,
    now_ref,
    prev_ref,
    sems,
):
    def fetch(k, which):
        src, dst = ((now_hbm, now_ref), (prev_hbm, prev_ref))[which]
        return pltpu.make_async_copy(src.at[:, k], dst.at[:, k], sems.at[which, k])

    def start(k, carry):
        for part in range(2):
            for which in range(2):
                fetch(k + 8 * part, which).start()
        return carry

    lax.fori_loop(0, 8, start, 0)
    lane, sub = iotas()
    first = first_ref[0]
    even = even_ref[0] == 1

    def put(at, north, south):
        lata_ref[pl.ds(at, 8), :] = jnp.where(even, south, north)
        latb_ref[pl.ds(at, 8), :] = jnp.where(even, north, south)

    base = pl.multiple_of(jnp.where(first == 1, 0, 8), 8)
    turn = jnp.where(first == 1, 0, 4)
    extra = jnp.where(first == 1, 4, 11)

    def levels(k, tiles):
        for part in range(2):
            for which in range(2):
                fetch(k + 8 * part, which).wait()
        for v in range(VARS):
            both = []
            for ref in (now_ref, prev_ref):
                pair = [
                    roll_subs(ref[v, k + 8 * part, pl.ds(base, 8), :], (4 * part + turn) % 8)
                    for part in range(2)
                ]
                both.append(jnp.where(sub < 4, pair[0], pair[1]))
            tile, old = both[0], roll_lanes(both[1], 64)
            row = jnp.where(
                sub < 4,
                jnp.broadcast_to(now_ref[v, k, pl.ds(extra, 1), :], (8, LANES)),
                jnp.broadcast_to(now_ref[v, k + 8, pl.ds(extra, 1), :], (8, LANES)),
            )
            at = pl.multiple_of((v * 8 + k) * 8, 8)
            east_ref[pl.ds(at, 8), :] = jnp.where(
                lane >= 64, tile, jnp.where(lane >= 32, old, roll_lanes(row, 32))
            )
            west_ref[pl.ds(at, 8), :] = jnp.where(
                lane < 64, tile, jnp.where(lane < 96, old, roll_lanes(row, 96))
            )
        tiles = list(tiles)
        for part in range(2):
            for v in range(VARS):
                at = (v % 2) * 64 + 4 * (k + 8 * part)
                mine = (lane >= at) & (lane < at + 4)
                for which, ref in enumerate((now_ref, prev_ref)):
                    for half in range(2):
                        x = ref[v, k + 8 * part, 8 * half : 8 * half + 8, :]
                        slot = which * 8 + half * 4 + v // 2
                        tiles[slot] = jnp.where(mine, roll_lanes(x, at + 2), tiles[slot])
        return tuple(tiles)

    tiles = lax.fori_loop(0, 8, levels, (jnp.zeros((8, LANES), f32),) * TILES_COLS)
    for i in range(TILES_COLS):
        at = 8 * (TILES_POLAR + i)
        west_ref[at : at + 8, :] = tiles[i]
        east_ref[at : at + 8, :] = tiles[i]

    def rows_now(g, carry):
        for v in range(VARS):
            north = None
            south = None
            for h in range(4):
                up = now_ref[v, g + 4 * h, 0:8, :]
                down = now_ref[v, g + 4 * h, 8:16, :]
                up = roll_subs(up, 2 * h) if h else up
                down = roll_subs(down, (2 * h + 2) % 8) if h != 3 else down
                mask = sub >= 2 * h
                north = up if h == 0 else jnp.where(mask, up, north)
                south = down if h == 0 else jnp.where(mask, down, south)
            at = pl.multiple_of((v * 4 + g) * 8, 8)
            put(at, north, south)
        return carry

    lax.fori_loop(0, 4, rows_now, 0)

    def rows_prev(g, carry):
        for v in range(VARS):
            north = None
            south = None
            for h in range(8):
                up = prev_ref[v, g + 2 * h, 0:8, :]
                down = prev_ref[v, g + 2 * h, 8:16, :]
                up = roll_subs(up, h) if h else up
                down = roll_subs(down, h + 1) if h != 7 else down
                mask = sub >= h
                north = up if h == 0 else jnp.where(mask, up, north)
                south = down if h == 0 else jnp.where(mask, down, south)
            at = pl.multiple_of((LAT_NOW + v * 2 + g) * 8, 8)
            put(at, north, south)
        return carry

    lax.fori_loop(0, 2, rows_prev, 0)


def prep_kernel(
    lon_ref,
    stride_ref,
    flen_ref,
    zc_ref,
    count_ref,
    listed_ref,
    w1_ref,
    shift_out,
    cz_out,
    mask_out,
    w1_out,
    zc_out,
):
    sub = lax.broadcasted_iota(jnp.int32, (ROWS, LANES), 0)
    tables = []
    for ref in (stride_ref, flen_ref, zc_ref):
        x = jnp.full((ROWS, LANES), ref[0])
        for j in range(1, ROWS):
            x = jnp.where(sub == j, ref[j], x)
        tables.append(x)
    shift_out[0:ROWS, :] = tables[0]
    shift_out[ROWS : 2 * ROWS, :] = tables[1]
    cz_out[...] = tables[2] * (1.0 / tables[0].astype(f32))
    zc_out[0:8, :] = jnp.broadcast_to(tables[2][0:1, :], (8, LANES))
    zc_out[8:16, :] = jnp.broadcast_to(tables[2][15:16, :], (8, LANES))

    listed = listed_ref[...]
    live = lax.broadcasted_iota(jnp.int32, (1, LISTED), 1) < count_ref[0, lon_ref[0]]
    row_hot = (listed // LANES == lax.broadcasted_iota(jnp.int32, (ROWS, LISTED), 0)) & live
    col_hot = listed % LANES == lax.broadcasted_iota(jnp.int32, (LANES, LISTED), 0)
    mask_out[...] = lax.dot_general(
        jnp.where(row_hot, 1.0, 0.0).astype(bf16),
        jnp.where(col_hot, 1.0, 0.0).astype(bf16),
        (((1,), (1,)), ((), ())),
        preferred_element_type=f32,
    )
    column = lax.broadcasted_iota(jnp.int32, (HID, VARS * ROWS), 1) % ROWS
    w1 = w1_ref[...]
    for r in range(ROWS):
        w1_out[r] = jnp.where(column == r, w1, 0.0).astype(bf16)


def shifts(amount):
    lane, _ = iotas()
    return (
        (lane + amount) % LANES,
        lane < amount,
        (lane - amount) % LANES,
        lane >= LANES - amount,
    )


def around(x, other, tab):
    lane, _ = iotas()
    if tab is None:
        return (
            roll_lanes(jnp.where(lane == 0, other, x), LANES - 1),
            roll_lanes(jnp.where(lane == LANES - 1, other, x), 1),
        )
    return (
        pick(jnp.where(tab[1], other, x), tab[0]),
        pick(jnp.where(tab[3], other, x), tab[2]),
    )


def merid_of(t0, t1, above, below):
    _, sub = iotas()
    u0, u1, d0, d1 = roll_subs(t0, 7), roll_subs(t1, 7), roll_subs(t0, 1), roll_subs(t1, 1)
    bottom = sub == 7
    top = sub == 0
    return (
        jnp.where(bottom, u1, u0) - jnp.where(top, above, d0),
        jnp.where(bottom, below, u1) - jnp.where(top, d0, d1),
    )


def tend(x, other, merid, cu, cv, fc, s_tab, m_tab):
    right, left = around(x, other, s_tab)
    zonal = right - left
    if m_tab is not None:
        right, left = around(x, other, m_tab)
    return fc * (right + left - 2.0 * x) - cu * zonal - cv * merid


def tables_of(shift_ref, polar):
    s_tab = shifts(shift_ref[8 * polar : 8 * polar + 8, :])
    m_tab = shifts(shift_ref[ROWS + 8 * polar : ROWS + 8 * polar + 8, :])
    return [(s_tab, m_tab) if h == polar else (None, None) for h in range(2)]


def step_kernel(
    first_ref,
    merid_ref,
    filter_ref,
    now_ref,
    prev_ref,
    fromwest_ref,
    fromeast_ref,
    shift_ref,
    cz_ref,
    new_ref,
    halo_ref,
    filtered_ref,
    wind_ref,
    pstar_ref,
):
    lane, sub = iotas()
    first = first_ref[0]
    west_cols = (lane % 4) < 2
    for i in range(TILES_COLS):
        at = 8 * (TILES_POLAR + i)
        pstar_ref[8 * i : 8 * i + 8, :] = jnp.where(
            west_cols, fromwest_ref[at : at + 8, :], fromeast_ref[at : at + 8, :]
        )
    edge = (lane < 2) | (lane >= 126)
    zero = jnp.zeros((8, LANES), f32)

    def take_step(polar):
        is_polar = (sub < 4) if polar == 0 else (sub >= 4)

        def level(k, carry):
            mc = merid_ref[k]
            fc = filter_ref[k]
            pol_at = 8 * (k % 8)
            pol_turn = (4 * polar + 8 - 4 * (k // 8)) % 8
            tabs = tables_of(shift_ref, polar)
            cz = [cz_ref[0:8, :], cz_ref[8:16, :]]

            def gather_tiles(v):
                group = v // 2
                back = 126 - (v % 2) * 64 - 4 * k
                cells = [now_ref[v, k, 0:8, :], now_ref[v, k, 8:16, :]]
                old = [prev_ref[v, k, 0:8, :], prev_ref[v, k, 8:16, :]]
                at = pl.multiple_of(v * 64 + pol_at, 8)
                te = fromeast_ref[pl.ds(at, 8), :]
                tw = fromwest_ref[pl.ds(at, 8), :]
                natural = roll_subs(jnp.where(lane < 64, te, tw), pol_turn)
                crossed = roll_subs(jnp.where(lane < 64, tw, te), pol_turn)
                near = jnp.where(lane < 64, roll_lanes(crossed, 32), roll_lanes(crossed, 96))
                strip = jnp.where(is_polar, natural, roll_subs(near, 4))
                strip_old = roll_lanes(crossed, 64)
                halo = []
                halo_old = []
                for half in range(2):
                    tile = 8 * (half * 4 + group)
                    x = roll_lanes(pstar_ref[tile : tile + 8, :], back)
                    halo.append(jnp.where(edge, x, strip) if half == polar else x)
                    x = roll_lanes(pstar_ref[tile + 64 : tile + 72, :], back)
                    halo_old.append(jnp.where(edge, x, strip_old) if half == polar else x)
                return cells, old, halo, halo_old

            def advance(v, tiles, cu_c, cv_c, cu_h, cv_h):
                cells, old, halo, halo_old = tiles
                md = merid_of(cells[0], cells[1], zero, zero)
                mh = merid_of(halo[0], halo[1], zero, zero)
                for h in range(2):
                    x, o = cells[h], halo[h]
                    rows = slice(8 * h, 8 * h + 8)
                    n = old[h] + tend(x, o, md[h], cu_c[h], cv_c[h], fc, *tabs[h])
                    new_ref[v, k, rows, :] = n
                    filtered_ref[v, k, rows, :] = x + 0.1 * (old[h] - 2.0 * x + n)
                    halo_ref[v, k, rows, :] = halo_old[h] + tend(
                        o, x, mh[h], cu_h[h], cv_h[h], fc, *tabs[h]
                    )

            u = gather_tiles(0)
            w = gather_tiles(1)
            cu_c = [cz[h] * u[0][h] for h in range(2)]
            cv_c = [mc * w[0][h] for h in range(2)]
            cu_h = [cz[h] * u[2][h] for h in range(2)]
            cv_h = [mc * w[2][h] for h in range(2)]
            for h in range(2):
                wind_ref[k, 8 * h : 8 * h + 8, :] = w[2][h]
            for v in range(VARS):
                tiles = u if v == 0 else w if v == 1 else gather_tiles(v)
                advance(v, tiles, cu_c, cv_c, cu_h, cv_h)
            return carry

        lax.fori_loop(0, LEV, level, 0)

    @pl.when(first == 1)
    def _():
        take_step(0)

    @pl.when(first != 1)
    def _():
        take_step(1)


def main_kernel(
    first_ref,
    even_ref,
    merid_ref,
    filter_ref,
    now_ref,
    new_ref,
    halo_ref,
    filtered_ref,
    wind_ref,
    froma_ref,
    fromb_ref,
    shift_ref,
    cz_ref,
    mask_ref,
    w1_ref,
    b1_ref,
    w2_ref,
    b2_ref,
    w3_ref,
    b3_ref,
    start_ref,
    prev_out,
    now_out,
    outp_ref,
    outn_ref,
    feats_ref,
    h2a_ref,
    h2b_ref,
    part_ref,
    sems,
    last_sem,
):
    lane, sub = iotas()
    first = first_ref[0]
    even = even_ref[0] == 1
    bottom = sub == 7
    top = sub == 0
    zero = jnp.zeros((8, LANES), f32)
    north_half = jnp.where(even, sub, 7 - sub) >= 4

    def outer(at):
        a = jnp.broadcast_to(froma_ref[at : at + 1, :], (8, LANES))
        b = jnp.broadcast_to(fromb_ref[at : at + 1, :], (8, LANES))
        return jnp.where(jnp.where(sub == 7, even_ref[0], 1 - even_ref[0]) == 1, b, a)

    def take_steps(polar):
        def level(k, carry):
            mc = merid_ref[k]
            fc = filter_ref[k]
            gn, hn = k % 4, k // 4
            gp, hp = k % 2, k // 2
            tabs = tables_of(shift_ref, polar)
            cz = [cz_ref[0:8, :], cz_ref[8:16, :], outer(LAT_ROWS - 4)]
            up_now, down_now = (14 - 2 * hn) % 8, (8 - 2 * hn) % 8
            up_old, down_old = 7 - hp, (8 - hp) % 8
            turn_now = (jnp.where(even, down_now, up_now), jnp.where(even, up_now, down_now))
            turn_old = (jnp.where(even, down_old, up_old), jnp.where(even, up_old, down_old))

            def outer_tiles(v):
                back = 126 - (v % 2) * 64 - 4 * k
                pair = []
                for at, turn in (
                    ((v * 4 + gn) * 8, turn_now),
                    ((LAT_NOW + v * 2 + gp) * 8, turn_old),
                ):
                    at = pl.multiple_of(at, 8)
                    a = roll_subs(froma_ref[pl.ds(at, 8), :], turn[0])
                    b = roll_subs(fromb_ref[pl.ds(at, 8), :], turn[1])
                    pair.append(jnp.where(north_half, b, a))
                return pair[0], pair[1], roll_lanes(outer(LAT_ROWS - 8 + v // 2), back)

            def first_step(v, tiles, cu_2, cv_2, cv_c, cv_h):
                t2, t2_old, t2_halo = tiles
                above = jnp.where(top, roll_subs(t2, 1), zero)
                below = jnp.where(bottom, roll_subs(t2, 7), zero)
                above_h = jnp.where(top, roll_subs(t2_halo, 1), zero)
                below_h = jnp.where(bottom, roll_subs(t2_halo, 7), zero)
                more = [cv_c[0] * above, -(cv_c[1] * below)]
                more_h = [cv_h[0] * above_h, -(cv_h[1] * below_h)]
                new = []
                new_halo = []
                filtered = []
                for h in range(2):
                    rows = slice(8 * h, 8 * h + 8)
                    new.append(new_ref[v, k, rows, :] + more[h])
                    filtered.append(filtered_ref[v, k, rows, :] + 0.1 * more[h])
                    new_halo.append(halo_ref[v, k, rows, :] + more_h[h])
                merid = jnp.where(
                    bottom, roll_subs(now_ref[v, k, 0:8, :], 7), roll_subs(t2, 7)
                ) - jnp.where(top, roll_subs(now_ref[v, k, 8:16, :], 1), roll_subs(t2, 1))
                new_t2 = t2_old + tend(t2, t2_halo, merid, cu_2, cv_2, fc, None, None)
                return new, new_halo, new_t2, filtered

            def second_step(v, stepped, cu, cv):
                new, new_halo, new_t2, filtered = stepped
                md = merid_of(new[0], new[1], roll_subs(new_t2, 1), roll_subs(new_t2, 7))
                both = []
                for h in range(2):
                    x = new[h]
                    n = filtered[h] + tend(x, new_halo[h], md[h], cu[h], cv[h], fc, *tabs[h])
                    outn_ref[v, k, 8 * h : 8 * h + 8, :] = n
                    outp_ref[v, k, 8 * h : 8 * h + 8, :] = x + 0.1 * (filtered[h] - 2.0 * x + n)
                    both.append(n)
                at = pl.multiple_of((k % 2) * LANES, LANES)
                feats_ref[k // 2, 16 * v : 16 * v + 16, pl.ds(at, LANES)] = jnp.concatenate(
                    both, axis=0
                ).astype(bf16)

            u = outer_tiles(0)
            w = outer_tiles(1)
            cu_2 = cz[2] * u[0]
            cv_2 = mc * w[0]
            cv_c = [mc * now_ref[1, k, 8 * h : 8 * h + 8, :] for h in range(2)]
            cv_h = [mc * wind_ref[k, 8 * h : 8 * h + 8, :] for h in range(2)]
            stepped_u = first_step(0, u, cu_2, cv_2, cv_c, cv_h)
            stepped_w = first_step(1, w, cu_2, cv_2, cv_c, cv_h)
            cu = [cz[h] * stepped_u[0][h] for h in range(2)]
            cv = [mc * stepped_w[0][h] for h in range(2)]
            second_step(0, stepped_u, cu, cv)
            second_step(1, stepped_w, cu, cv)
            for v in range(2, VARS):
                second_step(v, first_step(v, outer_tiles(v), cu_2, cv_2, cv_c, cv_h), cu, cv)
            pltpu.make_async_copy(outp_ref.at[:, k], prev_out.at[:, k], sems.at[k, 0]).start()
            pltpu.make_async_copy(outn_ref.at[0:2, k], now_out.at[0:2, k], sems.at[k, 1]).start()
            pltpu.make_async_copy(outn_ref.at[3:7, k], now_out.at[3:7, k], sems.at[k, 2]).start()
            return carry

        lax.fori_loop(0, NLEVELS, level, 0)

    @pl.when(first == 1)
    def _():
        take_steps(0)

    @pl.when(first != 1)
    def _():
        take_steps(1)

    start_sum = None
    for i in range(GPT // 8):
        t = jnp.exp2(-TAU_SCALE * start_ref[8 * i : 8 * i + 8, :])
        start_sum = t if start_sum is None else start_sum + t

    def hidden(r, p, dst):
        z = jnp.dot(w1_ref[r], feats_ref[p], preferred_element_type=f32)
        z = z + jnp.concatenate([b1_ref[...]] * 2, axis=1)
        h1 = (z * jnp.tanh(z) + z).astype(bf16)
        z = jnp.dot(w2_ref[...], h1, preferred_element_type=f32)
        z = z + jnp.concatenate([b2_ref[...]] * 2, axis=1)
        dst[p] = (z * jnp.tanh(z) + z).astype(bf16)

    def optics(at, width, p, src, total):
        y = jnp.dot(w3_ref[at : at + width, :], src[p], preferred_element_type=f32)
        for side in range(2):
            x = y[:, LANES * side : LANES * side + LANES] * LOG2E + b3_ref[at : at + width, :]
            e = jnp.exp2(jnp.minimum(x, 126.0))
            total = total + jnp.maximum(x, jnp.log2(1.0 + e))
            t = jnp.exp2(-TAU_SCALE * total)
            s = t[0:8]
            for i in range(1, width // 8):
                s = s + t[8 * i : 8 * i + 8]
            k = 2 * p + side
            part_ref[k] = s if at == 0 else part_ref[k] + s
        return total

    def phase(r, src, after, dst):
        done = 0
        turns = len(PARTS) * (LEV // 2)
        for n, (at, width) in enumerate(PARTS):
            total = start_ref[at : at + width, :]
            for p in range(LEV // 2):
                while done * turns < (LEV // 2) * (n * (LEV // 2) + p + 1):
                    hidden(after, done, dst)
                    done += 1
                total = optics(at, width, p, src, total)
        lit = mask_ref[pl.ds(r, 1), :] > 0.5
        before = start_sum
        for k in range(LEV):
            now = part_ref[k]
            heat = jnp.sum(before - now, axis=0, keepdims=True)
            before = now
            outn_ref[2, k, pl.ds(r, 1), :] = outn_ref[2, k, pl.ds(r, 1), :] + jnp.where(
                lit, heat, 0.0
            )

    def two_rows(i, carry):
        phase(2 * i, h2a_ref, 2 * i + 1, h2b_ref)
        phase(2 * i + 1, h2b_ref, jnp.minimum(2 * i + 2, ROWS - 1), h2a_ref)
        return carry

    for p in range(LEV // 2):
        hidden(0, p, h2a_ref)
    lax.fori_loop(0, ROWS // 2 if NETWORK else 0, two_rows, 0)
    last = pltpu.make_async_copy(outn_ref.at[2], now_out.at[2], last_sem)
    last.start()

    def drain(k, carry):
        pltpu.make_async_copy(outp_ref.at[:, k], prev_out.at[:, k], sems.at[k, 0]).wait()
        pltpu.make_async_copy(outn_ref.at[0:2, k], now_out.at[0:2, k], sems.at[k, 1]).wait()
        pltpu.make_async_copy(outn_ref.at[3:7, k], now_out.at[3:7, k], sems.at[k, 2]).wait()
        return carry

    lax.fori_loop(0, NLEVELS, drain, 0)
    last.wait()


VMEM = pl.BlockSpec(memory_space=pltpu.VMEM)
SMEM = pl.BlockSpec(memory_space=pltpu.SMEM)
ANY = pl.BlockSpec(memory_space=pl.ANY)
HBM = pl.BlockSpec(memory_space=pltpu.HBM)


def body(
    state_prev,
    state_now,
    stride_table,
    filter_len,
    zonal_coef,
    merid_coef,
    filter_coef,
    w_first,
    b_first,
    w_second,
    b_second,
    w_third,
    b_third,
    band_weight,
    sunlit_cols,
    sunlit_count,
):
    first = (lax.axis_index("lat") == 0).astype(jnp.int32).reshape(1)
    even = (lax.axis_index("lat") % 2 == 0).astype(jnp.int32).reshape(1)
    lon = lax.axis_index("lon").astype(jnp.int32).reshape(1)

    lon_shape = jax.ShapeDtypeStruct((LON_ROWS, LANES), f32)
    lat_shape = jax.ShapeDtypeStruct((LAT_ROWS, LANES), f32)
    state = jax.ShapeDtypeStruct(state_now.shape, f32)
    east, west, lata, latb = pl.pallas_call(
        pack_kernel,
        name="pack",
        out_shape=(lon_shape, lon_shape, lat_shape, lat_shape),
        in_specs=[SMEM, SMEM, HBM, HBM],
        out_specs=(VMEM,) * 4,
        scratch_shapes=[
            pltpu.VMEM(state_now.shape, f32),
            pltpu.VMEM(state_now.shape, f32),
            pltpu.SemaphoreType.DMA((2, LEV)),
        ],
        compiler_params=pltpu.CompilerParams(vmem_limit_bytes=16 << 20),
    )(
        first,
        even,
        pltpu.with_memory_space_constraint(state_now, pltpu.HBM),
        pltpu.with_memory_space_constraint(state_prev, pltpu.HBM),
    )

    def wide(vector):
        return jnp.broadcast_to(vector[:, None], (vector.shape[0], LANES))

    w1 = jnp.repeat(w_first.T.astype(f32) * 0.5, ROWS, axis=1)
    shift, cz, mask, w1, ends = pl.pallas_call(
        prep_kernel,
        name="prep",
        out_shape=(
            jax.ShapeDtypeStruct((2 * ROWS, LANES), jnp.int32),
            jax.ShapeDtypeStruct((ROWS, LANES), f32),
            jax.ShapeDtypeStruct((ROWS, LANES), f32),
            jax.ShapeDtypeStruct((ROWS, HID, VARS * ROWS), bf16),
            jax.ShapeDtypeStruct((ROWS, LANES), f32),
        ),
        in_specs=[SMEM] * 5 + [VMEM] * 2,
        out_specs=(VMEM,) * 5,
        compiler_params=pltpu.CompilerParams(vmem_limit_bytes=8 << 20),
    )(lon, stride_table, filter_len, zonal_coef, sunlit_count, sunlit_cols.reshape(1, LISTED), w1)
    w2 = (w_second.T.astype(f32) * 0.5).astype(bf16)
    w3 = w_third.T
    b1 = wide(b_first * 0.5)
    b2 = wide(b_second * 0.5)
    b3 = wide(b_third * LOG2E)
    start = wide(jnp.log2(band_weight) * (-1.0 / TAU_SCALE))

    nlon = lax.axis_size("lon")
    nlat = lax.axis_size("lat")
    fromwest = lax.ppermute(east, "lon", [(i, (i + 1) % nlon) for i in range(nlon)])
    fromeast = lax.ppermute(west, "lon", [((i + 1) % nlon, i) for i in range(nlon)])

    west_cols = (jnp.arange(LANES) % 4 < 2)[None, :]

    def corners(half, row):
        at = col_tile(0, half, 0)
        pieces = [
            x[at : at + 32].reshape(4, 8, LANES)[:, row] for x in (fromwest, fromeast)
        ]
        return jnp.where(west_cols, pieces[0], pieces[1])

    tail = (LAT_ROWS - 8, 0)
    lata = lax.dynamic_update_slice(lata, jnp.where(even == 1, ends[8:], ends[:8]), tail)
    latb = lax.dynamic_update_slice(latb, jnp.where(even == 1, ends[:8], ends[8:]), tail)
    north, south = corners(0, 0), corners(1, 7)
    lata = lax.dynamic_update_slice(lata, jnp.where(even == 1, south, north), (LAT_ROWS - 8, 0))
    latb = lax.dynamic_update_slice(latb, jnp.where(even == 1, north, south), (LAT_ROWS - 8, 0))
    (lata, latb, shift, cz, mask, w1, w2, w3, b1, b2, b3, start) = lax.optimization_barrier(
        (lata, latb, shift, cz, mask, w1, w2, w3, b1, b2, b3, start)
    )
    swap_a = [(i, i ^ 1) for i in range(nlat)]
    swap_b = [(i, i + 1 if i % 2 else i - 1) for i in range(1, nlat - 1)]
    froma = lax.ppermute(lata, "lat", swap_a)
    fromb = lax.ppermute(latb, "lat", swap_b)

    new, halo, filtered, wind = pl.pallas_call(
        step_kernel,
        name="step",
        out_shape=(state, state, state, jax.ShapeDtypeStruct((LEV, ROWS, LANES), f32)),
        in_specs=[SMEM] * 3 + [VMEM] * 6,
        out_specs=(VMEM,) * 4,
        scratch_shapes=[pltpu.VMEM((8 * TILES_COLS, LANES), f32)],
        cost_estimate=pl.CostEstimate(
            flops=20_000_000, bytes_accessed=24_000_000, transcendentals=0
        ),
        compiler_params=pltpu.CompilerParams(vmem_limit_bytes=STEPLIM << 20),
    )(
        first,
        merid_coef,
        filter_coef,
        state_now,
        state_prev,
        fromwest,
        fromeast,
        shift,
        cz,
    )

    prev_out, now_out = pl.pallas_call(
        main_kernel,
        name="main",
        out_shape=(state, state),
        in_specs=[SMEM] * 4 + [VMEM] * 17,
        out_specs=(ANY, ANY),
        scratch_shapes=[
            pltpu.VMEM(state_now.shape, f32),
            pltpu.VMEM(state_now.shape, f32),
            pltpu.VMEM((LEV // 2, VARS * ROWS, 2 * LANES), bf16),
            pltpu.VMEM((LEV // 2, HID, 2 * LANES), bf16),
            pltpu.VMEM((LEV // 2, HID, 2 * LANES), bf16),
            pltpu.VMEM((LEV, 8, LANES), f32),
            pltpu.SemaphoreType.DMA((LEV, 3)),
            pltpu.SemaphoreType.DMA,
        ],
        compiler_params=pltpu.CompilerParams(vmem_limit_bytes=MAINLIM << 20),
    )(
        first,
        even,
        merid_coef,
        filter_coef,
        state_now,
        new,
        halo,
        filtered,
        wind,
        froma,
        fromb,
        shift,
        cz,
        mask,
        w1,
        b1,
        w2,
        b2,
        w3,
        b3,
        start,
    )
    return prev_out, now_out


def solution(mesh):
    in_specs = (
        P(None, None, "lat", "lon"),
        P(None, None, "lat", "lon"),
        P("lat"),
        P("lat"),
        P("lat"),
        P(),
        P(),
        P(),
        P(),
        P(),
        P(),
        P(),
        P(),
        P(),
        P("lat", "lon", None),
        P("lat", None),
    )
    out_specs = (P(None, None, "lat", "lon"), P(None, None, "lat", "lon"))
    return jax.shard_map(body, mesh=mesh, in_specs=in_specs, out_specs=out_specs, check_vma=False)
```
